256 devices in a mesh: dp: 8 (over y, x_lo), mp: 32 (over z, x_hi, core).
Axes of the slice: x: 4 (x_hi: 2, x_lo: 2; x = x_hi * 2 + x_lo), y: 4, z: 8, core: 2. Of those that a mesh axis runs over, the one named last changes fastest.
Arguments:
- inputs: bfloat16 [4096, 1024], P('dp'), may hold values from -60 to 60
- norm_gain_vector: float32 [1024], replicated, may hold values from 0.5 to 1.5
- query_saved: bfloat16 [4096, 16384], P('dp', 'mp'), may hold values from -5 to 5
- key_saved: bfloat16 [4096, 16384], P('dp', 'mp'), may hold values from -2 to 2
- value_saved: bfloat16 [4096, 16384], P('dp', 'mp'), may hold values from -6 to 6
- w_query: bfloat16 [1024, 16384], P(None, 'mp'), may hold values from -0.1875 to 0.1875
- w_key: bfloat16 [1024, 16384], P(None, 'mp'), may hold values from -0.1875 to 0.1875
- w_value: bfloat16 [1024, 16384], P(None, 'mp'), may hold values from -0.1875 to 0.1875
- w_out: bfloat16 [16384, 1024], P('mp'), may hold values from -0.046875 to 0.046875
- output_gradient: bfloat16 [4096, 1024], P('dp'), may hold values from -4 to 4
Outputs:
- grad_inputs: bfloat16 [4096, 1024], P('dp')
- grad_w_query: bfloat16 [1024, 16384], P(None, 'mp')
- grad_w_key: bfloat16 [1024, 16384], P(None, 'mp')
- grad_w_value: bfloat16 [1024, 16384], P(None, 'mp')
- grad_w_out: bfloat16 [16384, 1024], P('mp')
- grad_gain: float32 [1024], replicated
The draws below stay inside these ranges and needn't reach their ends.
All inputs are finite; a program needn't handle non-finite values.
Results may differ from the reference program's by a relative error of at most 0.034.
Values may be sent and summed in bfloat16 or wider, within the bound.
No kernel may reach another device: no remote copies, remote signals or barrier semaphores. Data moves between devices by JAX's collectives and lax.ppermute only.
A program may use at most 64 MiB of HBM per device.

```python
import math
import jax
import jax.numpy as jnp
from jax import lax

D = 1024
HEADS = 128
HD = 128
SEQ = 512
INNER = 16384
TOKENS = 4096
N_DP = 8


def draw_inputs(key, part):
    first, second, third = jax.random.split(key, 3)
    base = jnp.clip(jax.random.normal(first, (TOKENS, D), jnp.float32), -6.0, 6.0)
    row_scale = jnp.exp(jax.random.uniform(second, (TOKENS, 1), jnp.float32, math.log(0.3), math.log(3.0)))
    col_scale = jnp.exp(jax.random.uniform(third, (1, D), jnp.float32, math.log(0.3), math.log(3.0)))
    return (base * row_scale * col_scale).astype(jnp.bfloat16)


def draw_pair(key):
    query_key = jax.random.fold_in(key, 101)
    key_key = jax.random.fold_in(key, 202)
    scale = HD ** (-0.5)
    queries = jnp.clip(jax.random.normal(query_key, (TOKENS, INNER), jnp.float32), -6.0, 6.0) * scale
    keys = jnp.clip(jax.random.normal(key_key, (TOKENS, INNER), jnp.float32), -6.0, 6.0) * scale
    return (queries.astype(jnp.bfloat16), keys.astype(jnp.bfloat16))


def draw_query_saved(key, part):
    return draw_pair(key)[0]


def draw_key_saved(key, part):
    return draw_pair(key)[1]


def steps_of(rng, extent, pieces, smallest, largest):
    def one(dim, parts):
        heights = jax.random.uniform(jax.random.fold_in(jax.random.fold_in(rng, 6), dim), (parts,), jnp.float32, smallest / len(pieces), largest / len(pieces))
        return jnp.repeat(jnp.exp(heights), extent[dim] // parts).reshape((-1,) + (1,) * (len(extent) - dim - 1))

    level = one(*pieces[0])
    for cut in pieces[1:]:
        level = level * one(*cut)
    return level


def gaussian(stream_key, shape, deviation, bound, shards=(), dtype=jnp.bfloat16):
    loudness = steps_of(stream_key, shape, shards, -0.22, 0.18) if shards else 1.0
    entries = jax.random.normal(stream_key, shape, jnp.float32) * deviation * loudness
    return jnp.minimum(jnp.maximum(entries, -bound), bound).astype(dtype)


def setup_inputs(seed: int = 0) -> dict:
    key_list = jax.random.split(jax.random.key(seed), 11)
    inputs = draw_inputs(jax.random.fold_in(key_list[10], 71), 0)
    norm_gain_vector = jnp.clip(1.0 + 0.1 * jax.random.normal(key_list[1], (D,), jnp.float32), 0.5, 1.5)
    query_saved = draw_query_saved(jax.random.fold_in(key_list[10], 71), 0)
    key_saved = draw_key_saved(jax.random.fold_in(key_list[10], 71), 0)
    value_saved = gaussian(key_list[4], (TOKENS, INNER), 1.0, 6.0, ((0, 8), (1, 32)))
    w_query = gaussian(key_list[5], (D, INNER), D ** -0.5, 0.1875, ((1, 32),))
    w_key = gaussian(key_list[6], (D, INNER), D ** -0.5, 0.1875, ((1, 32),))
    w_value = gaussian(key_list[7], (D, INNER), D ** -0.5, 0.1875, ((1, 32),))
    w_out = gaussian(key_list[8], (INNER, D), INNER ** -0.5, 0.046875, ((0, 32),))
    output_gradient = gaussian(key_list[9], (TOKENS, D), 0.25, 4.0, ((0, 8),))
    return dict(inputs=inputs, norm_gain_vector=norm_gain_vector, query_saved=query_saved, key_saved=key_saved, value_saved=value_saved, w_query=w_query, w_key=w_key, w_value=w_value, w_out=w_out, output_gradient=output_gradient)


def sequence_grads(block):
    rows, queries, keys_in, values, gradient_rows, gain_vector, w_query, w_key, w_value, w_out = block
    single_float_type = jnp.float32
    brain_float_half = jnp.bfloat16
    widened_rows = rows.astype(single_float_type)
    reciprocal_deviation = lax.rsqrt(lax.optimization_barrier(jnp.mean(widened_rows * widened_rows, axis=-1, keepdims=True)) + 1e-06)
    unit_input_rows = widened_rows * reciprocal_deviation
    normalized_rows = (unit_input_rows * gain_vector).astype(brain_float_half)
    query = queries.reshape(SEQ, HEADS, HD).astype(single_float_type)
    keys = keys_in.reshape(SEQ, HEADS, HD).astype(single_float_type)
    vals = values.reshape(SEQ, HEADS, HD).astype(single_float_type)
    scores = jnp.einsum('qhd,khd->hqk', query, keys)
    probs = jax.nn.softmax(scores, axis=-1)
    probs_low = probs.astype(brain_float_half)
    attended = jnp.einsum('hqk,khd->qhd', probs_low.astype(single_float_type), vals).astype(brain_float_half).reshape(SEQ, INNER)
    grad_att = jnp.dot(gradient_rows, w_out.T, preferred_element_type=single_float_type).astype(brain_float_half)
    part_out = jnp.dot(attended.T, gradient_rows, preferred_element_type=single_float_type)
    grad_att3 = grad_att.reshape(SEQ, HEADS, HD).astype(single_float_type)
    grad_val = jnp.einsum('hqk,qhd->khd', probs_low.astype(single_float_type), grad_att3).astype(brain_float_half)
    grad_prob = jnp.einsum('qhd,khd->hqk', grad_att3, vals)
    delta = lax.optimization_barrier(jnp.sum(probs * grad_prob, axis=-1, keepdims=True))
    grad_score = (probs * (grad_prob - delta)).astype(brain_float_half).astype(single_float_type)
    grad_query = jnp.einsum('hqk,khd->qhd', grad_score, keys).astype(brain_float_half).reshape(SEQ, INNER)
    grad_key = jnp.einsum('hqk,qhd->khd', grad_score, query).astype(brain_float_half).reshape(SEQ, INNER)
    grad_val = grad_val.reshape(SEQ, INNER)
    part_query = jnp.dot(normalized_rows.T, grad_query, preferred_element_type=single_float_type)
    part_key = jnp.dot(normalized_rows.T, grad_key, preferred_element_type=single_float_type)
    part_value = jnp.dot(normalized_rows.T, grad_val, preferred_element_type=single_float_type)
    normalized_gradient = jnp.dot(grad_query, w_query.T, preferred_element_type=single_float_type) + jnp.dot(grad_key, w_key.T, preferred_element_type=single_float_type) + jnp.dot(grad_val, w_value.T, preferred_element_type=single_float_type)
    scaled_gradient = normalized_gradient * gain_vector
    inner_product = lax.optimization_barrier(jnp.mean(scaled_gradient * unit_input_rows, axis=-1, keepdims=True))
    input_gradient = (gradient_rows.astype(single_float_type) + reciprocal_deviation * (scaled_gradient - unit_input_rows * inner_product)).astype(brain_float_half)
    partial_gain = lax.optimization_barrier(jnp.sum(normalized_gradient * unit_input_rows, axis=0))
    return (input_gradient, part_query.astype(brain_float_half), part_key.astype(brain_float_half), part_value.astype(brain_float_half), part_out.astype(brain_float_half), partial_gain.astype(brain_float_half))

def reference(inputs, norm_gain_vector, query_saved, key_saved, value_saved, w_query, w_key, w_value, w_out, output_gradient):

    def one(items):
        rows, queries, keys_in, values, gradient_rows = items
        return sequence_grads((rows, queries, keys_in, values, gradient_rows, norm_gain_vector, w_query, w_key, w_value, w_out))
    outs = lax.map(one, (inputs.reshape(N_DP, SEQ, D), query_saved.reshape(N_DP, SEQ, INNER), key_saved.reshape(N_DP, SEQ, INNER), value_saved.reshape(N_DP, SEQ, INNER), output_gradient.reshape(N_DP, SEQ, D)))
    grad_inputs = outs[0].reshape(TOKENS, D)
    grad_w_query = lax.optimization_barrier(jnp.sum(outs[1].astype(jnp.float32), axis=0)).astype(jnp.bfloat16)
    grad_w_key = lax.optimization_barrier(jnp.sum(outs[2].astype(jnp.float32), axis=0)).astype(jnp.bfloat16)
    grad_w_value = lax.optimization_barrier(jnp.sum(outs[3].astype(jnp.float32), axis=0)).astype(jnp.bfloat16)
    grad_w_out = lax.optimization_barrier(jnp.sum(outs[4].astype(jnp.float32), axis=0)).astype(jnp.bfloat16)
    grad_gain = lax.optimization_barrier(jnp.sum(outs[5].astype(jnp.float32), axis=0))
    return (grad_inputs, grad_w_query, grad_w_key, grad_w_value, grad_w_out, grad_gain)
```

```python
import jax
import jax.numpy as jnp
from jax import lax
from jax.sharding import PartitionSpec as P

HD = 128
F32 = jnp.float32
BF16 = jnp.bfloat16


def dp_pairs(flip):
    return [(y * 2 + x, (lambda t: t[0] * 2 + t[1])(flip(y, x))) for y in range(4) for x in range(2)]


def gray(z):
    return z ^ (z >> 1)


RING = {gray(z): z for z in range(8)}


def mp_pairs(flip):
    return [
        (z * 4 + h * 2 + c, (lambda t: t[0] * 4 + t[1] * 2 + t[2])(flip(z, h, c)))
        for z in range(8)
        for h in range(2)
        for c in range(2)
    ]


PAIRS = {
    "y1": ("dp", dp_pairs(lambda y, x: (y ^ 1, x))),
    "y3": ("dp", dp_pairs(lambda y, x: (3 - y, x))),
    "x": ("dp", dp_pairs(lambda y, x: (y, 1 - x))),
    "core": ("mp", mp_pairs(lambda z, h, c: (z, h, 1 - c))),
    "g0": ("mp", mp_pairs(lambda z, h, c: (RING[gray(z) ^ 1], h, c))),
    "g1": ("mp", mp_pairs(lambda z, h, c: (RING[gray(z) ^ 2], h, c))),
    "g2": ("mp", mp_pairs(lambda z, h, c: (RING[gray(z) ^ 4], h, c))),
    "xh": ("mp", mp_pairs(lambda z, h, c: (z, 1 - h, c))),
}


def swap(value, step):
    axis, pairs = PAIRS[step]
    return lax.ppermute(value, axis, pairs)


def bits():
    dp = lax.axis_index("dp")
    mp = lax.axis_index("mp")
    y, x = dp >> 1, dp & 1
    z, h, c = mp >> 2, (mp >> 1) & 1, mp & 1
    g = z ^ (z >> 1)
    return {
        "y1": (y ^ (y >> 1)) & 1,
        "y3": y >> 1,
        "x": x,
        "core": c,
        "g0": g & 1,
        "g1": (g >> 1) & 1,
        "g2": (g >> 2) & 1,
        "xh": h,
    }


def halve(value, step, bit, dtype=BF16):
    half = value.shape[0] // 2
    keep = lax.dynamic_slice_in_dim(value, bit * half, half, 0)
    send = lax.dynamic_slice_in_dim(value, (1 - bit) * half, half, 0)
    got = swap(send, step)
    return (keep.astype(F32) + got.astype(F32)).astype(dtype)


def double(value, step, bit):
    got = swap(value, step)
    low = bit == 0
    return jnp.concatenate([jnp.where(low, value, got), jnp.where(low, got, value)], axis=0)


def shards(
    inputs,
    norm_gain_vector,
    query_saved,
    key_saved,
    value_saved,
    w_query,
    w_key,
    w_value,
    w_out,
    output_gradient,
):
    length = inputs.shape[0]
    width = query_saved.shape[1]
    heads = width // HD
    bit = bits()
    rows = inputs.astype(F32)
    rstd = lax.rsqrt(jnp.mean(rows * rows, axis=-1, keepdims=True) + 1e-06)
    unit = rows * rstd
    normed = (unit * norm_gain_vector).astype(BF16)
    query = query_saved.reshape(length, heads, HD)
    keys = key_saved.reshape(length, heads, HD)
    values = value_saved.reshape(length, heads, HD)
    scores = jnp.einsum("qhd,khd->hqk", query, keys, preferred_element_type=F32)
    probs = jax.nn.softmax(scores, axis=-1)
    probs_low = probs.astype(BF16)
    attended = (
        jnp.einsum("hqk,khd->qhd", probs_low, values, preferred_element_type=F32)
        .astype(BF16)
        .reshape(length, width)
    )
    grad_att = jnp.einsum("td,id->ti", output_gradient, w_out, preferred_element_type=F32).astype(BF16)
    part_out = jnp.einsum("ti,td->id", attended, output_gradient, preferred_element_type=F32).astype(BF16)
    grad_att3 = grad_att.reshape(length, heads, HD)
    grad_val = (
        jnp.einsum("hqk,qhd->khd", probs_low, grad_att3, preferred_element_type=F32)
        .astype(BF16)
        .reshape(length, width)
    )
    grad_prob = jnp.einsum("qhd,khd->hqk", grad_att3, values, preferred_element_type=F32)
    delta = jnp.sum(probs * grad_prob, axis=-1, keepdims=True)
    grad_score = (probs * (grad_prob - delta)).astype(BF16)
    grad_query = (
        jnp.einsum("hqk,khd->qhd", grad_score, keys, preferred_element_type=F32)
        .astype(BF16)
        .reshape(length, width)
    )
    grad_key = (
        jnp.einsum("hqk,qhd->khd", grad_score, query, preferred_element_type=F32)
        .astype(BF16)
        .reshape(length, width)
    )
    part_query = jnp.einsum("td,ti->di", normed, grad_query, preferred_element_type=F32).astype(BF16)
    part_key = jnp.einsum("td,ti->di", normed, grad_key, preferred_element_type=F32).astype(BF16)
    part_value = jnp.einsum("td,ti->di", normed, grad_val, preferred_element_type=F32).astype(BF16)
    total = jnp.einsum("ti,di->td", grad_query, w_query, preferred_element_type=F32)
    total = total + jnp.einsum("ti,di->td", grad_key, w_key, preferred_element_type=F32)
    total = total + jnp.einsum("ti,di->td", grad_val, w_value, preferred_element_type=F32)

    gain = jnp.sum(total * unit, axis=0).reshape(8, 128)
    piece = total.astype(BF16)
    start = 0
    size = length
    for step in ("core", "g0", "g1", "g2", "xh"):
        size //= 2
        start = start + bit[step] * size
        piece = halve(piece, step, bit[step], F32 if step == "xh" else BF16)
    own_rows = lax.dynamic_slice_in_dim(inputs, start, size, 0).astype(F32)
    own_rstd = lax.rsqrt(jnp.mean(own_rows * own_rows, axis=-1, keepdims=True) + 1e-06)
    own_unit = own_rows * own_rstd
    own_gradient = lax.dynamic_slice_in_dim(output_gradient, start, size, 0).astype(F32)
    scaled = piece * norm_gain_vector
    inner = jnp.mean(scaled * own_unit, axis=-1, keepdims=True)
    grad_inputs = (own_gradient + own_rstd * (scaled - own_unit * inner)).astype(BF16)
    for step in ("xh", "g2", "g1", "g0", "core"):
        grad_inputs = double(grad_inputs, step, bit[step])

    for step in ("core", "g0", "g1", "g2", "xh", "x", "y1", "y3"):
        gain = gain + swap(gain, step)

    orders = (("x", "y1", "y3"), ("x", "y3", "y1"), ("y3", "y1", "x"), ("y1", "y3", "x"))
    outs = []
    for part, order in zip((part_query, part_key, part_value, part_out), orders):
        for step in order:
            part = halve(part, step, bit[step])
        for step in order[::-1]:
            part = double(part, step, bit[step])
        outs.append(part)
    return (grad_inputs, *outs, gain.reshape(-1))


def solution(mesh):
    return jax.shard_map(
        shards,
        mesh=mesh,
        in_specs=(
            P("dp", None),
            P(),
            P("dp", "mp"),
            P("dp", "mp"),
            P("dp", "mp"),
            P(None, "mp"),
            P(None, "mp"),
            P(None, "mp"),
            P("mp", None),
            P("dp", None),
        ),
        out_specs=(P("dp", None), P(None, "mp"), P(None, "mp"), P(None, "mp"), P("mp", None), P()),
        check_vma=False,
    )
```

```python
import functools

import jax
import jax.numpy as jnp
from jax import lax
from jax.experimental import pallas as pl
from jax.experimental.pallas import tpu as pltpu
from jax.sharding import PartitionSpec as P

HD = 128
F32 = jnp.float32
BF16 = jnp.bfloat16
EXTRA = 16


def gray(z):
    return z ^ (z >> 1)


RING = {gray(z): z for z in range(8)}


def dp_pairs(flip):
    return [(y * 2 + x, (lambda t: t[0] * 2 + t[1])(flip(y, x))) for y in range(4) for x in range(2)]


def mp_pairs(flip):
    return [
        (z * 4 + h * 2 + c, (lambda t: t[0] * 4 + t[1] * 2 + t[2])(flip(z, h, c)))
        for z in range(8)
        for h in range(2)
        for c in range(2)
    ]


PAIRS = {
    "y1": ("dp", dp_pairs(lambda y, x: (y ^ 1, x))),
    "y3": ("dp", dp_pairs(lambda y, x: (3 - y, x))),
    "x": ("dp", dp_pairs(lambda y, x: (y, 1 - x))),
    "core": ("mp", mp_pairs(lambda z, h, c: (z, h, 1 - c))),
    "g0": ("mp", mp_pairs(lambda z, h, c: (RING[gray(z) ^ 1], h, c))),
    "g1": ("mp", mp_pairs(lambda z, h, c: (RING[gray(z) ^ 2], h, c))),
    "g2": ("mp", mp_pairs(lambda z, h, c: (RING[gray(z) ^ 4], h, c))),
    "xh": ("mp", mp_pairs(lambda z, h, c: (z, 1 - h, c))),
}

ORDERS = (("y1", "y3", "x"), ("y3", "x", "y1"), ("x", "y1", "y3"))
PIECES = (
    (("out", 0, 8), ("value", 0, 3)),
    (("value", 3, 5), ("query", 0, 5)),
    (("query", 5, 3), ("key", 0, 8)),
)
UNIT = 16


def piece_rows(piece):
    return sum(count for _, _, count in piece) * UNIT


def swap(value, step):
    axis, pairs = PAIRS[step]
    return lax.ppermute(value, axis, pairs)


def codes():
    dp = lax.axis_index("dp").astype(jnp.int32)
    mp = lax.axis_index("mp").astype(jnp.int32)
    y, x = dp >> 1, dp & 1
    z, c = mp >> 2, mp & 1
    y1, y3 = (y ^ (y >> 1)) & 1, y >> 1
    g = z ^ (z >> 1)
    bit = {"y1": y1, "y3": y3, "x": x}
    piece = [bit[o[0]] * 4 + bit[o[1]] * 2 + bit[o[2]] for o in ORDERS]
    return jnp.stack([*piece, c * 4 + (g & 1) * 2 + ((g >> 1) & 1)])


def mm(a, b, ca, cb):
    return lax.dot_general(a, b, (((ca,), (cb,)), ((), ())), preferred_element_type=F32)


def split(g):
    high = g.astype(BF16)
    low = (g - high.astype(F32)).astype(BF16)
    return high, low


def joined(high, low):
    return high.astype(F32) + low.astype(F32)


def gain_rows(g):
    high, low = split(g)
    width = g.shape[1]
    row = lax.broadcasted_iota(jnp.int32, (EXTRA, width), 0)
    high = jnp.broadcast_to(high.astype(F32), (EXTRA, width))
    low = jnp.broadcast_to(low.astype(F32), (EXTRA, width))
    return jnp.where(row == 0, high, jnp.where(row == 1, low, 0.0)).astype(BF16)


def gain_of(rows):
    rows = rows.astype(F32)
    return rows[0:1] + rows[1:2]


def attention_kernel(q_ref, k_ref, v_ref, wo_ref, og_ref, att_ref, gq_ref, gk_ref, gv_ref):
    q, k, v = q_ref[...], k_ref[...], v_ref[...]
    scores = mm(q, k, 1, 1)
    top = jnp.max(scores, axis=-1, keepdims=True)
    e = jnp.exp(scores - top)
    probs = e * (1.0 / jnp.sum(e, axis=-1, keepdims=True))
    low = probs.astype(BF16)
    att_ref[...] = mm(low, v, 1, 0).astype(BF16)
    grad_att = mm(og_ref[...], wo_ref[...], 1, 1).astype(BF16)
    gv_ref[...] = mm(low, grad_att, 0, 0).astype(BF16)
    grad_prob = mm(grad_att, v, 1, 1)
    delta = jnp.sum(probs * grad_prob, axis=-1, keepdims=True)
    grad_score = (probs * (grad_prob - delta)).astype(BF16)
    gq_ref[...] = mm(grad_score, k, 1, 0).astype(BF16)
    gk_ref[...] = mm(grad_score, q, 0, 0).astype(BF16)


def attention(q, k, v, wo, og):
    length, width = q.shape
    depth = og.shape[1]
    column = pl.BlockSpec((length, HD), lambda h: (0, h))
    return pl.pallas_call(
        attention_kernel,
        grid=(width // HD,),
        in_specs=[
            column,
            column,
            column,
            pl.BlockSpec((HD, depth), lambda h: (h, 0)),
            pl.BlockSpec((length, depth), lambda h: (0, 0)),
        ],
        out_specs=[column] * 4,
        out_shape=[jax.ShapeDtypeStruct((length, width), BF16)] * 4,
        compiler_params=pltpu.CompilerParams(vmem_limit_bytes=20 << 20),
        cost_estimate=pl.CostEstimate(flops=6 << 30, bytes_accessed=8 << 20, transcendentals=1 << 20),
        name="attention",
    )(q, k, v, wo, og)


def norm_of(rows):
    rows = rows.astype(F32)
    rstd = lax.rsqrt(jnp.mean(rows * rows, axis=-1, keepdims=True) + 1e-06)
    return rows * rstd, rstd


def parts_kernel(code_ref, x_ref, gain_ref, og_ref, att_ref, gq_ref, gk_ref, gv_ref, *refs):
    outs, scratch = refs[:6], dict(zip(("out", "value", "query", "key"), refs[6:]))
    unit, _ = norm_of(x_ref[...])
    normed = (unit * gain_ref[...]).astype(BF16)
    scratch["out"][...] = mm(att_ref[...], og_ref[...], 0, 0).astype(BF16)
    scratch["value"][...] = mm(normed, gv_ref[...], 0, 0).astype(BF16)
    scratch["query"][...] = mm(normed, gq_ref[...], 0, 0).astype(BF16)
    scratch["key"][...] = mm(normed, gk_ref[...], 0, 0).astype(BF16)
    for i, piece in enumerate(PIECES):
        size = piece_rows(piece)
        for p in range(8):
            block = p ^ code_ref[i]
            dst = outs[2 * i] if p >= 4 else outs[2 * i + 1]
            at = (p % 4) * size
            for name, first, count in piece:
                if name == "out":
                    rows = pl.ds(pl.multiple_of(block * 64, 64), 64)
                    dst[pl.ds(at, 64), :] = scratch[name][rows, :512]
                    dst[pl.ds(at + 64, 64), :] = scratch[name][rows, 512:]
                else:
                    n = count * UNIT
                    rows = pl.ds(pl.multiple_of(block * 128 + first * UNIT, UNIT), n)
                    dst[pl.ds(at, n), :] = scratch[name][rows, :]
                at += count * UNIT


def whole(count):
    return [pl.BlockSpec(memory_space=pltpu.VMEM)] * count


SCALARS = pl.BlockSpec(memory_space=pltpu.SMEM)


def parts(code, inputs, gain, og, att, gq, gk, gv):
    depth, width = inputs.shape[1], gq.shape[1]
    shapes = []
    for piece in PIECES:
        shapes += [jax.ShapeDtypeStruct((4 * piece_rows(piece), width), BF16)] * 2
    return pl.pallas_call(
        parts_kernel,
        in_specs=[SCALARS, *whole(7)],
        out_specs=whole(6),
        out_shape=shapes,
        scratch_shapes=[pltpu.VMEM((width, depth), BF16)] + [pltpu.VMEM((depth, width), BF16)] * 3,
        compiler_params=pltpu.CompilerParams(vmem_limit_bytes=24 << 20),
        cost_estimate=pl.CostEstimate(flops=2 << 30, bytes_accessed=8 << 20, transcendentals=0),
        name="parts",
    )(code, inputs, gain, og, att, gq, gk, gv)


def total_kernel(code_ref, x_ref, gq_ref, gk_ref, gv_ref, wq_ref, wk_ref, wv_ref, send_ref, keep_ref, gain_ref, low_ref):
    total = mm(gq_ref[...], wq_ref[...], 1, 1)
    total = total + mm(gk_ref[...], wk_ref[...], 1, 1)
    total = total + mm(gv_ref[...], wv_ref[...], 1, 1)
    unit, _ = norm_of(x_ref[...])
    g = jnp.sum(total * unit, axis=0, keepdims=True)
    low_ref[...] = total.astype(BF16)
    for p in range(8):
        block = p ^ code_ref[3]
        dst = send_ref if p >= 4 else keep_ref
        dst[pl.ds((p % 4) * 64, 64), :] = low_ref[pl.ds(pl.multiple_of(block * 64, 64), 64), :]
    send_ref[pl.ds(256, EXTRA), :] = gain_rows(g)
    gain_ref[...] = joined(*split(g))


def total_share(code, inputs, gq, gk, gv, wq, wk, wv):
    length, depth = inputs.shape
    half = length // 2
    return pl.pallas_call(
        total_kernel,
        in_specs=[SCALARS, *whole(7)],
        out_specs=whole(3),
        out_shape=[
            jax.ShapeDtypeStruct((half + EXTRA, depth), BF16),
            jax.ShapeDtypeStruct((half, depth), BF16),
            jax.ShapeDtypeStruct((1, depth), F32),
        ],
        scratch_shapes=[pltpu.VMEM((length, depth), BF16)],
        compiler_params=pltpu.CompilerParams(vmem_limit_bytes=20 << 20),
        cost_estimate=pl.CostEstimate(flops=2 << 30, bytes_accessed=8 << 20, transcendentals=0),
        name="total_share",
    )(code, inputs, gq, gk, gv, wq, wk, wv)


def mp_step_kernel(rows, first, gain_ref, *refs):
    *sums, last, send_ref, out_ref = refs
    value = sums[0][pl.ds(first, rows), :].astype(F32)
    for ref in (*sums[1:], last):
        value = value + ref[pl.ds(first, rows), :].astype(F32)
    send_ref[pl.ds(0, rows), :] = value.astype(BF16)
    got = last[pl.ds(last.shape[0] - EXTRA, EXTRA), :]
    g = gain_ref[...] + gain_of(got)
    send_ref[pl.ds(rows, EXTRA), :] = gain_rows(g)
    out_ref[...] = joined(*split(g))


def mp_step(gain, sums, rows, first):
    depth = gain.shape[1]
    return pl.pallas_call(
        functools.partial(mp_step_kernel, rows, first),
        in_specs=whole(1 + len(sums)),
        out_specs=whole(2),
        out_shape=[jax.ShapeDtypeStruct((rows + EXTRA, depth), BF16), jax.ShapeDtypeStruct((1, depth), F32)],
        compiler_params=pltpu.CompilerParams(vmem_limit_bytes=4 << 20),
        cost_estimate=pl.CostEstimate(flops=1 << 20, bytes_accessed=2 << 20, transcendentals=0),
        name="mp_step",
    )(gain, *sums)


def rows_kernel(code_ref, x_ref, og_ref, weight_ref, gain_ref, mine_ref, got_ref, out_ref, sum_ref):
    n = out_ref.shape[0]
    gradient = mine_ref[pl.ds(0, n), :].astype(F32) + got_ref[pl.ds(0, n), :].astype(F32)
    unit, rstd = norm_of(x_ref[...])
    scaled = gradient * weight_ref[...]
    inner = jnp.mean(scaled * unit, axis=-1, keepdims=True)
    out_ref[...] = (og_ref[...].astype(F32) + rstd * (scaled - unit * inner)).astype(BF16)
    sum_ref[...] = gain_ref[...] + gain_of(got_ref[pl.ds(n, EXTRA), :])


def own_rows(code, inputs, og, weight, gain, mine, got):
    n, depth = mine.shape[0] - EXTRA, mine.shape[1]

    def fixed(shape):
        return pl.BlockSpec(shape, lambda i, c: (0, 0))

    row = pl.BlockSpec((n, depth), lambda i, c: (c[3], 0))
    return pl.pallas_call(
        rows_kernel,
        grid_spec=pltpu.PrefetchScalarGridSpec(
            num_scalar_prefetch=1,
            grid=(1,),
            in_specs=[row, row, fixed((1, depth)), fixed((1, depth)), fixed(mine.shape), fixed(got.shape)],
            out_specs=[fixed((n, depth)), fixed((1, depth))],
        ),
        out_shape=[jax.ShapeDtypeStruct((n, depth), BF16), jax.ShapeDtypeStruct((1, depth), F32)],
        compiler_params=pltpu.CompilerParams(vmem_limit_bytes=4 << 20),
        cost_estimate=pl.CostEstimate(flops=1 << 20, bytes_accessed=1 << 20, transcendentals=0),
        name="own_rows",
    )(code, inputs, og, weight, gain, mine, got)


def finish_kernel(code_ref, *refs):
    halves, outs = refs[:8], refs[8:]
    grad_inputs_ref = outs[0]
    named = dict(zip(("query", "key", "value", "out"), outs[1:]))
    for p in range(8):
        block = p ^ code_ref[3]
        src = halves[7] if p >= 4 else halves[6]
        grad_inputs_ref[pl.ds(pl.multiple_of(block * 64, 64), 64), :] = src[pl.ds((p % 4) * 64, 64), :]
    for i, piece in enumerate(PIECES):
        size = piece_rows(piece)
        for p in range(8):
            block = p ^ code_ref[i]
            src = halves[2 * i + 1] if p >= 4 else halves[2 * i]
            at = (p % 4) * size
            for name, first, count in piece:
                if name == "out":
                    rows = pl.ds(pl.multiple_of(block * 64, 64), 64)
                    named[name][rows, :512] = src[pl.ds(at, 64), :]
                    named[name][rows, 512:] = src[pl.ds(at + 64, 64), :]
                else:
                    n = count * UNIT
                    rows = pl.ds(pl.multiple_of(block * 128 + first * UNIT, UNIT), n)
                    named[name][rows, :] = src[pl.ds(at, n), :]
                at += count * UNIT


def finish(code, halves, length, depth, width):
    return pl.pallas_call(
        finish_kernel,
        in_specs=[SCALARS, *whole(8)],
        out_specs=whole(5),
        out_shape=[
            jax.ShapeDtypeStruct((length, depth), BF16),
            *[jax.ShapeDtypeStruct((depth, width), BF16)] * 3,
            jax.ShapeDtypeStruct((width, depth), BF16),
        ],
        compiler_params=pltpu.CompilerParams(vmem_limit_bytes=14 << 20),
        cost_estimate=pl.CostEstimate(flops=1 << 20, bytes_accessed=10 << 20, transcendentals=0),
        name="finish",
    )(code, *halves)


def plus(*values):
    total = values[0].astype(F32)
    for value in values[1:]:
        total = total + value.astype(F32)
    return total.astype(BF16)


def shards(
    inputs,
    norm_gain_vector,
    query_saved,
    key_saved,
    value_saved,
    w_query,
    w_key,
    w_value,
    w_out,
    output_gradient,
):
    length, depth = inputs.shape
    width = query_saved.shape[1]
    code = codes()
    weight = norm_gain_vector.reshape(1, depth)
    att, gq, gk, gv = attention(query_saved, key_saved, value_saved, w_out, output_gradient)
    pieces = parts(code, inputs, weight, output_gradient, att, gq, gk, gv)
    m_send, m_keep, gain = total_share(code, inputs, gq, gk, gv, w_query, w_key, w_value)

    sends, keeps = pieces[0::2], pieces[1::2]
    sizes = [piece_rows(piece) for piece in PIECES]
    first = [swap(s, o[0]) for s, o in zip(sends, ORDERS)]
    r1 = swap(m_send, "core")
    send, gain = mp_step(gain, (m_keep, r1), 128, 128)
    r2 = swap(send, "g0")
    second = [
        swap(plus(k[2 * n :], r[2 * n :]), o[1]) for k, r, o, n in zip(keeps, first, ORDERS, sizes)
    ]
    send, gain = mp_step(gain, (m_keep, r1, r2), 64, 64)
    r3 = swap(send, "g1")
    third = [
        swap(plus(k[n : 2 * n], r[n : 2 * n], s[n:]), o[2])
        for k, r, s, o, n in zip(keeps, first, second, ORDERS, sizes)
    ]
    send, gain = mp_step(gain, (m_keep, r1, r2, r3), 64, 0)
    r4 = swap(send, "g2")
    own = [plus(k[:n], r[:n], s[:n], t) for k, r, s, t, n in zip(keeps, first, second, third, sizes)]
    back = [swap(v, o[2]) for v, o in zip(own, ORDERS)]
    send, gain = mp_step(gain, (send, r4), 64, 0)
    r5 = swap(send, "xh")
    rows, gain = own_rows(code, inputs, output_gradient, weight, gain, send, r5)
    quarter = [jnp.concatenate([v, b]) for v, b in zip(own, back)]
    back = [swap(v, o[1]) for v, o in zip(quarter, ORDERS)]
    half = [jnp.concatenate([v, b]) for v, b in zip(quarter, back)]
    last = [swap(v, o[0]) for v, o in zip(half, ORDERS)]
    for step in ("g1", "g0"):
        rows = jnp.concatenate([rows, swap(rows, step)])
    rows_last = swap(rows, "core")
    for step in ("x", "y1", "y3"):
        gain = gain + swap(gain, step)
    halves = [v for pair in zip(half, last) for v in pair] + [rows, rows_last]
    outs = finish(code, halves, length, depth, width)
    return (*outs, gain.reshape(depth))


def solution(mesh):
    return jax.shard_map(
        shards,
        mesh=mesh,
        in_specs=(
            P("dp", None),
            P(),
            P("dp", "mp"),
            P("dp", "mp"),
            P("dp", "mp"),
            P(None, "mp"),
            P(None, "mp"),
            P(None, "mp"),
            P("mp", None),
            P("dp", None),
        ),
        out_specs=(P("dp", None), P(None, "mp"), P(None, "mp"), P(None, "mp"), P("mp", None), P()),
        check_vma=False,
    )
```

```python
import functools

import jax
import jax.numpy as jnp
from jax import lax
from jax.experimental import pallas as pl
from jax.experimental.pallas import tpu as pltpu
from jax.sharding import PartitionSpec as P

HD = 128
F32 = jnp.float32
BF16 = jnp.bfloat16
EXTRA = 16


def gray(z):
    return z ^ (z >> 1)


RING = {gray(z): z for z in range(8)}


def dp_pairs(flip):
    return [(y * 2 + x, (lambda t: t[0] * 2 + t[1])(flip(y, x))) for y in range(4) for x in range(2)]


def mp_pairs(flip):
    return [
        (z * 4 + h * 2 + c, (lambda t: t[0] * 4 + t[1] * 2 + t[2])(flip(z, h, c)))
        for z in range(8)
        for h in range(2)
        for c in range(2)
    ]


PAIRS = {
    "y1": ("dp", dp_pairs(lambda y, x: (y ^ 1, x))),
    "y3": ("dp", dp_pairs(lambda y, x: (3 - y, x))),
    "x": ("dp", dp_pairs(lambda y, x: (y, 1 - x))),
    "core": ("mp", mp_pairs(lambda z, h, c: (z, h, 1 - c))),
    "g0": ("mp", mp_pairs(lambda z, h, c: (RING[gray(z) ^ 1], h, c))),
    "g1": ("mp", mp_pairs(lambda z, h, c: (RING[gray(z) ^ 2], h, c))),
    "g2": ("mp", mp_pairs(lambda z, h, c: (RING[gray(z) ^ 4], h, c))),
    "xh": ("mp", mp_pairs(lambda z, h, c: (z, 1 - h, c))),
}

ORDERS = (("y1", "y3", "x"), ("y3", "x", "y1"), ("x", "y1", "y3"))
PIECES = (
    (("out", 0, 8), ("value", 0, 3)),
    (("value", 3, 5), ("query", 0, 5)),
    (("query", 5, 3), ("key", 0, 8)),
)
UNIT = 16


def piece_rows(piece):
    return sum(count for _, _, count in piece) * UNIT


def swap(value, step):
    axis, pairs = PAIRS[step]
    return lax.ppermute(value, axis, pairs)


def position():
    return jnp.stack([lax.axis_index("dp").astype(jnp.int32), lax.axis_index("mp").astype(jnp.int32)])


def piece_code(where, i):
    dp = where[0]
    y, x = dp >> 1, dp & 1
    bit = {"y1": (y ^ (y >> 1)) & 1, "y3": y >> 1, "x": x}
    return bit[ORDERS[i][0]] * 4 + bit[ORDERS[i][1]] * 2


def row_code(where):
    mp = where[1]
    z, c = mp >> 2, mp & 1
    g = z ^ (z >> 1)
    return c * 4 + (g & 1) * 2 + ((g >> 1) & 1)


def mm(a, b, ca, cb):
    return lax.dot_general(a, b, (((ca,), (cb,)), ((), ())), preferred_element_type=F32)


def split(g):
    high = g.astype(BF16)
    low = (g - high.astype(F32)).astype(BF16)
    return high, low


def joined(high, low):
    return high.astype(F32) + low.astype(F32)


def gain_rows(g):
    high, low = split(g)
    width = g.shape[1]
    row = lax.broadcasted_iota(jnp.int32, (EXTRA, width), 0)
    high = jnp.broadcast_to(high.astype(F32), (EXTRA, width))
    low = jnp.broadcast_to(low.astype(F32), (EXTRA, width))
    return jnp.where(row == 0, high, jnp.where(row == 1, low, 0.0)).astype(BF16)


def gain_of(rows):
    rows = rows.astype(F32)
    return rows[0:1] + rows[1:2]


def norm_of(rows):
    rows = rows.astype(F32)
    rstd = lax.rsqrt(jnp.mean(rows * rows, axis=-1, keepdims=True) + 1e-06)
    return rows * rstd, rstd


def whole(count):
    return [pl.BlockSpec(memory_space=pltpu.VMEM)] * count


SCALARS = pl.BlockSpec(memory_space=pltpu.SMEM)


def front_kernel(where, gain_ref, *refs):
    sources, refs = refs[:6], refs[6:]
    outs, refs = refs[:6], refs[6:]
    (gq, gk, gv), refs = refs[:3], refs[3:]
    copied, refs = refs[:6], refs[6:]
    (att, grad_att), refs = refs[:2], refs[2:]
    scratch, sem = dict(zip(("out", "value", "query", "key"), refs[:4])), refs[4]
    copies = [pltpu.make_async_copy(a, b, sem.at[i]) for i, (a, b) in enumerate(zip(sources, copied))]
    for copy in copies:
        copy.start()
    og, wo, q_all, k_all, v_all, x = copied
    copies[0].wait()
    copies[1].wait()
    grad_att[...] = mm(og[...], wo[...], 1, 1).astype(BF16)
    for copy in copies[2:]:
        copy.wait()
    for h in range(q_all.shape[1] // HD):
        col = pl.ds(h * HD, HD)
        q, k, v, ga = q_all[:, col], k_all[:, col], v_all[:, col], grad_att[:, col]
        scores = mm(q, k, 1, 1)
        top = jnp.max(scores, axis=-1, keepdims=True)
        e = jnp.exp(scores - top)
        probs = e * (1.0 / jnp.sum(e, axis=-1, keepdims=True))
        low = probs.astype(BF16)
        att[:, col] = mm(low, v, 1, 0).astype(BF16)
        grad_prob = mm(ga, v, 1, 1)
        delta = jnp.sum(probs * grad_prob, axis=-1, keepdims=True)
        grad_score = (probs * (grad_prob - delta)).astype(BF16)
        gq[:, col] = mm(grad_score, k, 1, 0).astype(BF16)
        gv[col, :] = mm(ga, low, 0, 0).astype(BF16)
        gk[col, :] = mm(q, grad_score, 0, 0).astype(BF16)
    scratch["out"][...] = mm(att[...], og[...], 0, 0).astype(BF16)
    unit, _ = norm_of(x[...])
    normed = (unit * gain_ref[...]).astype(BF16)
    scratch["value"][...] = mm(normed, gv[...], 0, 1).astype(BF16)
    scratch["query"][...] = mm(normed, gq[...], 0, 0).astype(BF16)
    scratch["key"][...] = mm(normed, gk[...], 0, 1).astype(BF16)
    for i, piece in enumerate(PIECES):
        code = piece_code(where, i)
        size = piece_rows(piece)
        for p in range(8):
            dst = outs[2 * i] if p >= 4 else outs[2 * i + 1]
            for at, src, rows in spans(piece, p, p ^ code, size):
                if src == "out":
                    dst[pl.ds(at, 64), :] = scratch[src][rows, :512]
                    dst[pl.ds(at + 64, 64), :] = scratch[src][rows, 512:]
                else:
                    dst[pl.ds(at, rows.size), :] = scratch[src][rows, :]


def spans(piece, p, block, size):
    at = (p % 4) * size
    for name, first, count in piece:
        if name == "out":
            yield at, name, pl.ds(pl.multiple_of(block * 64, 64), 64)
        else:
            yield at, name, pl.ds(pl.multiple_of(block * 128 + first * UNIT, UNIT), count * UNIT)
        at += count * UNIT


def front(where, weight, og, wo, q, k, v, x):
    (length, depth), width = x.shape, q.shape[1]
    shapes = []
    for piece in PIECES:
        shapes += [jax.ShapeDtypeStruct((4 * piece_rows(piece), width), BF16)] * 2
    shapes += [jax.ShapeDtypeStruct((length, width), BF16)] + [jax.ShapeDtypeStruct((width, length), BF16)] * 2
    sources = [pltpu.with_memory_space_constraint(a, pltpu.HBM) for a in (og, wo, q, k, v, x)]
    return pl.pallas_call(
        front_kernel,
        in_specs=[SCALARS, *whole(1), *[pl.BlockSpec(memory_space=pltpu.HBM)] * 6],
        out_specs=whole(9),
        out_shape=shapes,
        scratch_shapes=[
            *[pltpu.VMEM(a.shape, BF16) for a in (og, wo, q, k, v, x)],
            *[pltpu.VMEM((length, width), BF16)] * 2,
            pltpu.VMEM((width, depth), BF16),
            *[pltpu.VMEM((depth, width), BF16)] * 3,
            pltpu.SemaphoreType.DMA((6,)),
        ],
        compiler_params=pltpu.CompilerParams(vmem_limit_bytes=40 << 20),
        cost_estimate=pl.CostEstimate(flops=8 << 30, bytes_accessed=16 << 20, transcendentals=1 << 20),
        name="front",
    )(where, weight, *sources)


def total_kernel(where, x_ref, gq_ref, gk_ref, gv_ref, wq_ref, wk_ref, wv_ref, send_ref, keep_ref, gain_ref, low_ref):
    total = mm(gq_ref[...], wq_ref[...], 1, 1)
    total = total + mm(gk_ref[...], wk_ref[...], 0, 1)
    total = total + mm(gv_ref[...], wv_ref[...], 0, 1)
    unit, _ = norm_of(x_ref[...])
    g = jnp.sum(total * unit, axis=0, keepdims=True)
    low_ref[...] = total.astype(BF16)
    for p in range(8):
        block = p ^ row_code(where)
        dst = send_ref if p >= 4 else keep_ref
        dst[pl.ds((p % 4) * 64, 64), :] = low_ref[pl.ds(pl.multiple_of(block * 64, 64), 64), :]
    send_ref[pl.ds(256, EXTRA), :] = gain_rows(g)
    gain_ref[...] = joined(*split(g))


def total_share(where, inputs, gq, gk, gv, wq, wk, wv):
    length, depth = inputs.shape
    half = length // 2
    return pl.pallas_call(
        total_kernel,
        in_specs=[SCALARS, *whole(7)],
        out_specs=whole(3),
        out_shape=[
            jax.ShapeDtypeStruct((half + EXTRA, depth), BF16),
            jax.ShapeDtypeStruct((half, depth), BF16),
            jax.ShapeDtypeStruct((1, depth), F32),
        ],
        scratch_shapes=[pltpu.VMEM((length, depth), BF16)],
        compiler_params=pltpu.CompilerParams(vmem_limit_bytes=20 << 20),
        cost_estimate=pl.CostEstimate(flops=2 << 30, bytes_accessed=8 << 20, transcendentals=0),
        name="total_share",
    )(where, inputs, gq, gk, gv, wq, wk, wv)


def mp_step_kernel(rows, first, gain_ref, *refs):
    *sums, last, send_ref, out_ref = refs
    value = sums[0][pl.ds(first, rows), :].astype(F32)
    for ref in (*sums[1:], last):
        value = value + ref[pl.ds(first, rows), :].astype(F32)
    send_ref[pl.ds(0, rows), :] = value.astype(BF16)
    got = last[pl.ds(last.shape[0] - EXTRA, EXTRA), :]
    g = gain_ref[...] + gain_of(got)
    send_ref[pl.ds(rows, EXTRA), :] = gain_rows(g)
    out_ref[...] = joined(*split(g))


def mp_step(gain, sums, rows, first):
    depth = gain.shape[1]
    return pl.pallas_call(
        functools.partial(mp_step_kernel, rows, first),
        in_specs=whole(1 + len(sums)),
        out_specs=whole(2),
        out_shape=[jax.ShapeDtypeStruct((rows + EXTRA, depth), BF16), jax.ShapeDtypeStruct((1, depth), F32)],
        compiler_params=pltpu.CompilerParams(vmem_limit_bytes=4 << 20),
        cost_estimate=pl.CostEstimate(flops=1 << 10, bytes_accessed=1 << 10, transcendentals=0),
        name="mp_step",
    )(gain, *sums)


def rows_kernel(where, x_ref, og_ref, weight_ref, gain_ref, mine_ref, got_ref, out_ref, sum_ref):
    n = out_ref.shape[0]
    gradient = mine_ref[pl.ds(0, n), :].astype(F32) + got_ref[pl.ds(0, n), :].astype(F32)
    unit, rstd = norm_of(x_ref[...])
    scaled = gradient * weight_ref[...]
    inner = jnp.mean(scaled * unit, axis=-1, keepdims=True)
    out_ref[...] = (og_ref[...].astype(F32) + rstd * (scaled - unit * inner)).astype(BF16)
    g = gain_ref[...] + gain_of(got_ref[pl.ds(n, EXTRA), :])
    for j in range(8):
        for i in range(8):
            sum_ref[i, pl.ds(j, 1), :] = g[:, j * 128 : (j + 1) * 128]


def own_rows(where, inputs, og, weight, gain, mine, got):
    n, depth = mine.shape[0] - EXTRA, mine.shape[1]

    def fixed(shape):
        return pl.BlockSpec(shape, lambda i, c: (0, 0))

    row = pl.BlockSpec((n, depth), lambda i, c: (row_code(c), 0))
    return pl.pallas_call(
        rows_kernel,
        grid_spec=pltpu.PrefetchScalarGridSpec(
            num_scalar_prefetch=1,
            grid=(1,),
            in_specs=[row, row, fixed((1, depth)), fixed((1, depth)), fixed(mine.shape), fixed(got.shape)],
            out_specs=[fixed((n, depth)), pl.BlockSpec((8, 8, 128), lambda i, c: (0, 0, 0))],
        ),
        out_shape=[jax.ShapeDtypeStruct((n, depth), BF16), jax.ShapeDtypeStruct((8, 8, 128), F32)],
        compiler_params=pltpu.CompilerParams(vmem_limit_bytes=4 << 20),
        cost_estimate=pl.CostEstimate(flops=1 << 10, bytes_accessed=1 << 10, transcendentals=0),
        name="own_rows",
    )(where, inputs, og, weight, gain, mine, got)


ANYWHERE = pl.BlockSpec(memory_space=pl.ANY)


def place_kernel(late, where, *refs):
    halves, outs, sem = refs[:3], refs[-5:-1], refs[-1]
    named = dict(zip(("query", "key", "value", "out"), outs))
    copies = []
    for i, piece in enumerate(PIECES):
        code = piece_code(where, i)
        for p in range(4 * late, 4 * late + 4):
            for at, name, rows in spans(piece, p, p ^ code, piece_rows(piece)):
                if name == "out":
                    pairs = [(at, 64, named[name].at[rows, pl.ds(0, 512)]), (at + 64, 64, named[name].at[rows, pl.ds(512, 512)])]
                else:
                    pairs = [(at, rows.size, named[name].at[rows, :])]
                for first, n, dst in pairs:
                    copy = pltpu.make_async_copy(halves[i].at[pl.ds(first, n), :], dst, sem.at[len(copies)])
                    copy.start()
                    copies.append(copy)
    for copy in copies:
        copy.wait()


def place(late, where, halves, outs, depth, width):
    shapes = [jax.ShapeDtypeStruct((depth, width), BF16)] * 3 + [jax.ShapeDtypeStruct((width, depth), BF16)]
    return pl.pallas_call(
        functools.partial(place_kernel, late),
        in_specs=[SCALARS, *[ANYWHERE] * (3 + len(outs))],
        out_specs=[ANYWHERE] * 4,
        out_shape=shapes,
        scratch_shapes=[pltpu.SemaphoreType.DMA((28,))],
        input_output_aliases={4 + i: i for i in range(len(outs))},
        compiler_params=pltpu.CompilerParams(vmem_limit_bytes=1 << 20),
        cost_estimate=pl.CostEstimate(flops=1 << 10, bytes_accessed=4 << 20, transcendentals=0),
        name="place_late" if late else "place_early",
    )(where, *halves, *outs)


def place_rows_kernel(where, low_ref, high_ref, out_ref, sem):
    code = row_code(where)
    copies = []
    for p in range(8):
        src = high_ref if p >= 4 else low_ref
        rows = pl.ds(pl.multiple_of((p ^ code) * 64, 64), 64)
        copy = pltpu.make_async_copy(src.at[pl.ds((p % 4) * 64, 64), :], out_ref.at[rows, :], sem.at[p])
        copy.start()
        copies.append(copy)
    for copy in copies:
        copy.wait()


def place_rows(where, low, high):
    return pl.pallas_call(
        place_rows_kernel,
        in_specs=[SCALARS, ANYWHERE, ANYWHERE],
        out_specs=ANYWHERE,
        out_shape=jax.ShapeDtypeStruct((2 * low.shape[0], low.shape[1]), BF16),
        scratch_shapes=[pltpu.SemaphoreType.DMA((8,))],
        compiler_params=pltpu.CompilerParams(vmem_limit_bytes=1 << 20),
        cost_estimate=pl.CostEstimate(flops=1 << 10, bytes_accessed=2 << 20, transcendentals=0),
        name="place_rows",
    )(where, low, high)


def plus(*values):
    total = values[0].astype(F32)
    for value in values[1:]:
        total = total + value.astype(F32)
    return total.astype(BF16)


def shards(
    inputs,
    norm_gain_vector,
    query_saved,
    key_saved,
    value_saved,
    w_query,
    w_key,
    w_value,
    w_out,
    output_gradient,
):
    length, depth = inputs.shape
    width = query_saved.shape[1]
    where = position()
    weight = norm_gain_vector.reshape(1, depth)
    *pieces, gq, gk, gv = front(where, weight, output_gradient, w_out, query_saved, key_saved, value_saved, inputs)
    m_send, m_keep, gain = total_share(where, inputs, gq, gk, gv, w_query, w_key, w_value)

    sends, keeps = pieces[0::2], pieces[1::2]
    sizes = [piece_rows(piece) for piece in PIECES]
    first = [swap(s, o[0]) for s, o in zip(sends, ORDERS)]
    r1 = swap(m_send, "core")
    send, gain = mp_step(gain, (m_keep, r1), 128, 128)
    r2 = swap(send, "g0")
    second = [
        swap(plus(k[2 * n :], r[2 * n :]), o[1]) for k, r, o, n in zip(keeps, first, ORDERS, sizes)
    ]
    send, gain = mp_step(gain, (m_keep, r1, r2), 64, 64)
    r3 = swap(send, "g1")
    mine = [plus(k[: 2 * n], r[: 2 * n], s) for k, r, s, n in zip(keeps, first, second, sizes)]
    third = [swap(v, o[2]) for v, o in zip(mine, ORDERS)]
    send, gain = mp_step(gain, (m_keep, r1, r2, r3), 64, 0)
    r4 = swap(send, "g2")
    quarter = [plus(v, t) for v, t in zip(mine, third)]
    send, gain = mp_step(gain, (send, r4), 64, 0)
    r5 = swap(send, "xh")
    rows, gains = own_rows(where, inputs, output_gradient, weight, gain, send, r5)
    gains = lax.all_to_all(gains, "dp", 0, 0)
    back = [swap(v, o[1]) for v, o in zip(quarter, ORDERS)]
    half = [jnp.concatenate([v, b]) for v, b in zip(quarter, back)]
    *half, gains = lax.optimization_barrier((*half, gains))
    last = [swap(v, o[0]) for v, o in zip(half, ORDERS)]
    outs = place(0, where, half, (), depth, width)
    for step in ("g1", "g0"):
        rows = jnp.concatenate([rows, swap(rows, step)])
    grad_inputs = place_rows(where, rows, swap(rows, "core"))
    outs = place(1, where, last, outs, depth, width)
    return (grad_inputs, *outs, jnp.sum(gains, axis=0).reshape(depth))


def solution(mesh):
    return jax.shard_map(
        shards,
        mesh=mesh,
        in_specs=(
            P("dp", None),
            P(),
            P("dp", "mp"),
            P("dp", "mp"),
            P("dp", "mp"),
            P(None, "mp"),
            P(None, "mp"),
            P(None, "mp"),
            P("mp", None),
            P("dp", None),
        ),
        out_specs=(P("dp", None), P(None, "mp"), P(None, "mp"), P(None, "mp"), P("mp", None), P()),
        check_vma=False,
    )
```

```python
import functools

import jax
import jax.numpy as jnp
from jax import lax
from jax.experimental import pallas as pl
from jax.experimental.pallas import tpu as pltpu
from jax.sharding import PartitionSpec as P

HD = 128
F32 = jnp.float32
BF16 = jnp.bfloat16
EXTRA = 16


def gray(z):
    return z ^ (z >> 1)


RING = {gray(z): z for z in range(8)}


def dp_pairs(flip):
    return [(y * 2 + x, (lambda t: t[0] * 2 + t[1])(flip(y, x))) for y in range(4) for x in range(2)]


def mp_pairs(flip):
    return [
        (z * 4 + h * 2 + c, (lambda t: t[0] * 4 + t[1] * 2 + t[2])(flip(z, h, c)))
        for z in range(8)
        for h in range(2)
        for c in range(2)
    ]


PAIRS = {
    "y1": ("dp", dp_pairs(lambda y, x: (y ^ 1, x))),
    "y3": ("dp", dp_pairs(lambda y, x: (3 - y, x))),
    "x": ("dp", dp_pairs(lambda y, x: (y, 1 - x))),
    "core": ("mp", mp_pairs(lambda z, h, c: (z, h, 1 - c))),
    "g0": ("mp", mp_pairs(lambda z, h, c: (RING[gray(z) ^ 1], h, c))),
    "g1": ("mp", mp_pairs(lambda z, h, c: (RING[gray(z) ^ 2], h, c))),
    "g2": ("mp", mp_pairs(lambda z, h, c: (RING[gray(z) ^ 4], h, c))),
    "xh": ("mp", mp_pairs(lambda z, h, c: (z, 1 - h, c))),
}

ORDERS = (("y1", "y3", "x"), ("y3", "x", "y1"), ("x", "y1", "y3"))
PIECES = (
    (("out", 0, 8), ("value", 0, 3)),
    (("value", 3, 5), ("query", 0, 5)),
    (("query", 5, 3), ("key", 0, 8)),
)
UNIT = 16


def piece_rows(piece):
    return sum(count for _, _, count in piece) * UNIT


def swap(value, step):
    axis, pairs = PAIRS[step]
    return lax.ppermute(value, axis, pairs)


def position():
    return jnp.stack([lax.axis_index("dp").astype(jnp.int32), lax.axis_index("mp").astype(jnp.int32)])


def piece_code(where, i):
    dp = where[0]
    y, x = dp >> 1, dp & 1
    bit = {"y1": (y ^ (y >> 1)) & 1, "y3": y >> 1, "x": x}
    return bit[ORDERS[i][0]] * 4 + bit[ORDERS[i][1]] * 2


def row_code(where):
    mp = where[1]
    z, c = mp >> 2, mp & 1
    g = z ^ (z >> 1)
    return c * 4 + (g & 1) * 2 + ((g >> 1) & 1)


def mm(a, b, ca, cb):
    return lax.dot_general(a, b, (((ca,), (cb,)), ((), ())), preferred_element_type=F32)


def split(g):
    high = g.astype(BF16)
    low = (g - high.astype(F32)).astype(BF16)
    return high, low


def joined(high, low):
    return high.astype(F32) + low.astype(F32)


def gain_rows(g):
    high, low = split(g)
    width = g.shape[1]
    row = lax.broadcasted_iota(jnp.int32, (EXTRA, width), 0)
    high = jnp.broadcast_to(high.astype(F32), (EXTRA, width))
    low = jnp.broadcast_to(low.astype(F32), (EXTRA, width))
    return jnp.where(row == 0, high, jnp.where(row == 1, low, 0.0)).astype(BF16)


def gain_of(rows):
    rows = rows.astype(F32)
    return rows[0:1] + rows[1:2]


def norm_of(rows):
    rows = rows.astype(F32)
    rstd = lax.rsqrt(jnp.mean(rows * rows, axis=-1, keepdims=True) + 1e-06)
    return rows * rstd, rstd


def whole(count):
    return [pl.BlockSpec(memory_space=pltpu.VMEM)] * count


SCALARS = pl.BlockSpec(memory_space=pltpu.SMEM)


def front_kernel(where, *refs):
    sources, refs = refs[:7], refs[7:]
    outs, refs = refs[:6], refs[6:]
    (gq, gk, gv), refs = refs[:3], refs[3:]
    copied, refs = refs[:7], refs[7:]
    (att, grad_att), refs = refs[:2], refs[2:]
    scratch, sem = dict(zip(("out", "value", "query", "key"), refs[:4])), refs[4]
    copies = [pltpu.make_async_copy(a, b, sem.at[i]) for i, (a, b) in enumerate(zip(sources, copied))]
    for copy in copies:
        copy.start()
    og, wo, q_all, k_all, v_all, x, gain_ref = copied
    copies[0].wait()
    copies[1].wait()
    grad_att[...] = mm(og[...], wo[...], 1, 1).astype(BF16)
    for copy in copies[2:]:
        copy.wait()
    for h in range(q_all.shape[1] // HD):
        col = pl.ds(h * HD, HD)
        q, k, v, ga = q_all[:, col], k_all[:, col], v_all[:, col], grad_att[:, col]
        scores = mm(q, k, 1, 1)
        top = jnp.max(scores, axis=-1, keepdims=True)
        e = jnp.exp(scores - top)
        probs = e * (1.0 / jnp.sum(e, axis=-1, keepdims=True))
        low = probs.astype(BF16)
        att[:, col] = mm(low, v, 1, 0).astype(BF16)
        grad_prob = mm(ga, v, 1, 1)
        delta = jnp.sum(probs * grad_prob, axis=-1, keepdims=True)
        grad_score = (probs * (grad_prob - delta)).astype(BF16)
        gq[:, col] = mm(grad_score, k, 1, 0).astype(BF16)
        gv[col, :] = mm(ga, low, 0, 0).astype(BF16)
        gk[col, :] = mm(q, grad_score, 0, 0).astype(BF16)
    scratch["out"][...] = mm(att[...], og[...], 0, 0).astype(BF16)
    unit, _ = norm_of(x[...])
    normed = (unit * gain_ref[...]).astype(BF16)
    scratch["value"][...] = mm(normed, gv[...], 0, 1).astype(BF16)
    scratch["query"][...] = mm(normed, gq[...], 0, 0).astype(BF16)
    scratch["key"][...] = mm(normed, gk[...], 0, 1).astype(BF16)
    for i, piece in enumerate(PIECES):
        code = piece_code(where, i)
        size = piece_rows(piece)
        for p in range(8):
            dst = outs[2 * i] if p >= 4 else outs[2 * i + 1]
            for at, src, rows in spans(piece, p, p ^ code, size):
                if src == "out":
                    dst[pl.ds(at, 64), :] = scratch[src][rows, :512]
                    dst[pl.ds(at + 64, 64), :] = scratch[src][rows, 512:]
                else:
                    dst[pl.ds(at, rows.size), :] = scratch[src][rows, :]


def spans(piece, p, block, size):
    at = (p % 4) * size
    for name, first, count in piece:
        if name == "out":
            yield at, name, pl.ds(pl.multiple_of(block * 64, 64), 64)
        else:
            yield at, name, pl.ds(pl.multiple_of(block * 128 + first * UNIT, UNIT), count * UNIT)
        at += count * UNIT


def front(where, weight, og, wo, q, k, v, x):
    (length, depth), width = x.shape, q.shape[1]
    shapes = []
    for piece in PIECES:
        shapes += [jax.ShapeDtypeStruct((4 * piece_rows(piece), width), BF16)] * 2
    shapes += [jax.ShapeDtypeStruct((length, width), BF16)] + [jax.ShapeDtypeStruct((width, length), BF16)] * 2
    sources = [pltpu.with_memory_space_constraint(a, pltpu.HBM) for a in (og, wo, q, k, v, x, weight)]
    return pl.pallas_call(
        front_kernel,
        in_specs=[SCALARS, *[pl.BlockSpec(memory_space=pltpu.HBM)] * 7],
        out_specs=whole(9),
        out_shape=shapes,
        scratch_shapes=[
            *[pltpu.VMEM(a.shape, a.dtype) for a in (og, wo, q, k, v, x, weight)],
            *[pltpu.VMEM((length, width), BF16)] * 2,
            pltpu.VMEM((width, depth), BF16),
            *[pltpu.VMEM((depth, width), BF16)] * 3,
            pltpu.SemaphoreType.DMA((7,)),
        ],
        compiler_params=pltpu.CompilerParams(vmem_limit_bytes=40 << 20),
        cost_estimate=pl.CostEstimate(flops=8 << 30, bytes_accessed=16 << 20, transcendentals=1 << 20),
        name="front",
    )(where, *sources)


def total_kernel(where, x_ref, gq_ref, gk_ref, gv_ref, wq_ref, wk_ref, wv_ref, send_ref, keep_ref, gain_ref, low_ref):
    total = mm(gq_ref[...], wq_ref[...], 1, 1)
    total = total + mm(gk_ref[...], wk_ref[...], 0, 1)
    total = total + mm(gv_ref[...], wv_ref[...], 0, 1)
    unit, _ = norm_of(x_ref[...])
    g = jnp.sum(total * unit, axis=0, keepdims=True)
    low_ref[...] = total.astype(BF16)
    for p in range(8):
        block = p ^ row_code(where)
        dst = send_ref if p >= 4 else keep_ref
        dst[pl.ds((p % 4) * 64, 64), :] = low_ref[pl.ds(pl.multiple_of(block * 64, 64), 64), :]
    send_ref[pl.ds(256, EXTRA), :] = gain_rows(g)
    gain_ref[...] = joined(*split(g))


def total_share(where, inputs, gq, gk, gv, wq, wk, wv):
    length, depth = inputs.shape
    half = length // 2
    return pl.pallas_call(
        total_kernel,
        in_specs=[SCALARS, *whole(7)],
        out_specs=whole(3),
        out_shape=[
            jax.ShapeDtypeStruct((half + EXTRA, depth), BF16),
            jax.ShapeDtypeStruct((half, depth), BF16),
            jax.ShapeDtypeStruct((1, depth), F32),
        ],
        scratch_shapes=[pltpu.VMEM((length, depth), BF16)],
        compiler_params=pltpu.CompilerParams(vmem_limit_bytes=20 << 20),
        cost_estimate=pl.CostEstimate(flops=2 << 30, bytes_accessed=8 << 20, transcendentals=0),
        name="total_share",
    )(where, inputs, gq, gk, gv, wq, wk, wv)


def mp_step_kernel(rows, first, ties, gain_ref, *refs):
    *sums, last = refs[: -2 - ties]
    send_ref, out_ref = refs[-2:]
    value = sums[0][pl.ds(first, rows), :].astype(F32)
    for ref in (*sums[1:], last):
        value = value + ref[pl.ds(first, rows), :].astype(F32)
    send_ref[pl.ds(0, rows), :] = value.astype(BF16)
    got = last[pl.ds(last.shape[0] - EXTRA, EXTRA), :]
    g = gain_ref[...] + gain_of(got)
    send_ref[pl.ds(rows, EXTRA), :] = gain_rows(g)
    out_ref[...] = joined(*split(g))


def mp_step(gain, sums, rows, first, ties=()):
    depth = gain.shape[1]
    return pl.pallas_call(
        functools.partial(mp_step_kernel, rows, first, len(ties)),
        in_specs=[*whole(1 + len(sums)), *[ANYWHERE] * len(ties)],
        out_specs=whole(2),
        out_shape=[jax.ShapeDtypeStruct((rows + EXTRA, depth), BF16), jax.ShapeDtypeStruct((1, depth), F32)],
        compiler_params=pltpu.CompilerParams(vmem_limit_bytes=4 << 20),
        cost_estimate=pl.CostEstimate(flops=1 << 10, bytes_accessed=1 << 10, transcendentals=0),
        name="mp_step",
    )(gain, *sums, *ties)


def rows_kernel(where, x_ref, og_ref, weight_ref, gain_ref, mine_ref, got_ref, *refs):
    out_ref, sum_ref = refs[-2:]
    n = out_ref.shape[0]
    gradient = mine_ref[pl.ds(0, n), :].astype(F32) + got_ref[pl.ds(0, n), :].astype(F32)
    unit, rstd = norm_of(x_ref[...])
    scaled = gradient * weight_ref[...]
    inner = jnp.mean(scaled * unit, axis=-1, keepdims=True)
    out_ref[...] = (og_ref[...].astype(F32) + rstd * (scaled - unit * inner)).astype(BF16)
    g = gain_ref[...] + gain_of(got_ref[pl.ds(n, EXTRA), :])
    for j in range(8):
        for i in range(8):
            sum_ref[i, pl.ds(j, 1), :] = g[:, j * 128 : (j + 1) * 128]


def own_rows(where, inputs, og, weight, gain, mine, got, ties):
    n, depth = mine.shape[0] - EXTRA, mine.shape[1]

    def fixed(shape):
        return pl.BlockSpec(shape, lambda i, c: (0, 0))

    row = pl.BlockSpec((n, depth), lambda i, c: (row_code(c), 0))
    return pl.pallas_call(
        rows_kernel,
        grid_spec=pltpu.PrefetchScalarGridSpec(
            num_scalar_prefetch=1,
            grid=(1,),
            in_specs=[row, row, fixed((1, depth)), fixed((1, depth)), fixed(mine.shape), fixed(got.shape), *[ANYWHERE] * len(ties)],
            out_specs=[fixed((n, depth)), pl.BlockSpec((8, 8, 128), lambda i, c: (0, 0, 0))],
        ),
        out_shape=[jax.ShapeDtypeStruct((n, depth), BF16), jax.ShapeDtypeStruct((8, 8, 128), F32)],
        compiler_params=pltpu.CompilerParams(vmem_limit_bytes=4 << 20),
        cost_estimate=pl.CostEstimate(flops=1 << 10, bytes_accessed=1 << 10, transcendentals=0),
        name="own_rows",
    )(where, inputs, og, weight, gain, mine, got, *ties)


ANYWHERE = pl.BlockSpec(memory_space=pl.ANY)


def place_kernel(late, where, *refs):
    halves, sem = refs[:3], refs[-1]
    outs = refs[7:11] if late else refs[3:7]
    if not late:
        refs[7][...] = jnp.zeros(refs[7].shape, F32)
    named = dict(zip(("query", "key", "value", "out"), outs))
    copies = []
    for i, piece in enumerate(PIECES):
        code = piece_code(where, i)
        for p in range(4 * late, 4 * late + 4):
            for at, name, rows in spans(piece, p, p ^ code, piece_rows(piece)):
                if name == "out":
                    pairs = [(at, 64, named[name].at[rows, pl.ds(0, 512)]), (at + 64, 64, named[name].at[rows, pl.ds(512, 512)])]
                else:
                    pairs = [(at, rows.size, named[name].at[rows, :])]
                for first, n, dst in pairs:
                    copy = pltpu.make_async_copy(halves[i].at[pl.ds(first, n), :], dst, sem.at[len(copies)])
                    copy.start()
                    copies.append(copy)
    for copy in copies:
        copy.wait()


def place(late, where, halves, outs, depth, width):
    shapes = [jax.ShapeDtypeStruct((depth, width), BF16)] * 3 + [jax.ShapeDtypeStruct((width, depth), BF16)]
    return pl.pallas_call(
        functools.partial(place_kernel, late),
        in_specs=[SCALARS, *whole(3), *[ANYWHERE] * len(outs)],
        out_specs=[ANYWHERE] * 4 + whole(1 - late),
        out_shape=shapes + [jax.ShapeDtypeStruct((8, 128), F32)] * (1 - late),
        scratch_shapes=[pltpu.SemaphoreType.DMA((28,))],
        input_output_aliases={4 + i: i for i in range(len(outs))},
        compiler_params=pltpu.CompilerParams(vmem_limit_bytes=4 << 20),
        cost_estimate=pl.CostEstimate(flops=(1 << 36) if late else (1 << 10), bytes_accessed=1 << 10, transcendentals=0),
        name="place_late" if late else "place_early",
    )(where, *halves, *outs)


def place_rows_kernel(where, low_ref, high_ref, out_ref, sem):
    code = row_code(where)
    copies = []
    for p in range(8):
        src = high_ref if p >= 4 else low_ref
        rows = pl.ds(pl.multiple_of((p ^ code) * 64, 64), 64)
        copy = pltpu.make_async_copy(src.at[pl.ds((p % 4) * 64, 64), :], out_ref.at[rows, :], sem.at[p])
        copy.start()
        copies.append(copy)
    for copy in copies:
        copy.wait()


def place_rows(where, low, high):
    return pl.pallas_call(
        place_rows_kernel,
        in_specs=[SCALARS, *whole(2)],
        out_specs=ANYWHERE,
        out_shape=jax.ShapeDtypeStruct((2 * low.shape[0], low.shape[1]), BF16),
        scratch_shapes=[pltpu.SemaphoreType.DMA((8,))],
        compiler_params=pltpu.CompilerParams(vmem_limit_bytes=4 << 20),
        cost_estimate=pl.CostEstimate(flops=1 << 10, bytes_accessed=2 << 20, transcendentals=0),
        name="place_rows",
    )(where, low, high)


def plus(*values):
    total = values[0].astype(F32)
    for value in values[1:]:
        total = total + value.astype(F32)
    return total.astype(BF16)


def after(value, first):
    return lax.optimization_barrier((value, *first))[0]


def shards(
    inputs,
    norm_gain_vector,
    query_saved,
    key_saved,
    value_saved,
    w_query,
    w_key,
    w_value,
    w_out,
    output_gradient,
):
    length, depth = inputs.shape
    width = query_saved.shape[1]
    where = position()
    weight = norm_gain_vector.reshape(1, depth)
    *pieces, gq, gk, gv = front(where, weight, output_gradient, w_out, query_saved, key_saved, value_saved, inputs)
    m_send, m_keep, gain = total_share(where, inputs, gq, gk, gv, w_query, w_key, w_value)

    sends, keeps = pieces[0::2], pieces[1::2]
    sizes = [piece_rows(piece) for piece in PIECES]
    first = [swap(s, o[0]) for s, o in zip(sends, ORDERS)]
    r1 = swap(m_send, "core")
    send, gain = mp_step(gain, (m_keep, r1), 128, 128)
    r2 = swap(send, "g0")
    second = [plus(k[2 * n :], r[2 * n :]) for k, r, n in zip(keeps, first, sizes)]
    send, gain = mp_step(gain, (m_keep, r1, r2), 64, 64, second)
    second = [swap(v, o[1]) for v, o in zip(second, ORDERS)]
    r3 = swap(send, "g1")
    mine = [plus(k[: 2 * n], r[: 2 * n], s) for k, r, s, n in zip(keeps, first, second, sizes)]
    third = [swap(v, o[2]) for v, o in zip(mine, ORDERS)]
    send, gain = mp_step(gain, (m_keep, r1, r2, r3), 64, 0, mine)
    r4 = swap(send, "g2")
    quarter = [plus(v, t) for v, t in zip(mine, third)]
    back = [swap(v, o[1]) for v, o in zip(quarter, ORDERS)]
    half = [jnp.concatenate([v, b]) for v, b in zip(quarter, back)]
    last = [swap(v, o[0]) for v, o in zip(half, ORDERS)]
    send, gain = mp_step(gain, (send, r4), 64, 0, quarter)
    r5 = swap(send, "xh")
    rows, gains = own_rows(where, inputs, output_gradient, weight, gain, send, r5, half)
    *outs, placed = place(0, where, half, (), depth, width)
    for step in ("g1", "g0"):
        rows = jnp.concatenate([rows, swap(rows, step)])
    gains = lax.all_to_all(gains + placed, "dp", 0, 0)
    rows = after(rows, last)
    grad_inputs = place_rows(where, rows, swap(rows, "core"))
    outs = place(1, where, last, outs, depth, width)
    return (grad_inputs, *outs, jnp.sum(gains, axis=0).reshape(depth))


def solution(mesh):
    return jax.shard_map(
        shards,
        mesh=mesh,
        in_specs=(
            P("dp", None),
            P(),
            P("dp", "mp"),
            P("dp", "mp"),
            P("dp", "mp"),
            P(None, "mp"),
            P(None, "mp"),
            P(None, "mp"),
            P("mp", None),
            P("dp", None),
        ),
        out_specs=(P("dp", None), P(None, "mp"), P(None, "mp"), P(None, "mp"), P("mp", None), P()),
        check_vma=False,
    )
```

```python
import functools

import jax
import jax.numpy as jnp
from jax import lax
from jax.experimental import pallas as pl
from jax.experimental.pallas import tpu as pltpu
from jax.sharding import PartitionSpec as P

HD = 128
F32 = jnp.float32
BF16 = jnp.bfloat16
EXTRA = 16


def gray(z):
    return z ^ (z >> 1)


RING = {gray(z): z for z in range(8)}


def dp_pairs(flip):
    return [(y * 2 + x, (lambda t: t[0] * 2 + t[1])(flip(y, x))) for y in range(4) for x in range(2)]


def mp_pairs(flip):
    return [
        (z * 4 + h * 2 + c, (lambda t: t[0] * 4 + t[1] * 2 + t[2])(flip(z, h, c)))
        for z in range(8)
        for h in range(2)
        for c in range(2)
    ]


PAIRS = {
    "y1": ("dp", dp_pairs(lambda y, x: (y ^ 1, x))),
    "y3": ("dp", dp_pairs(lambda y, x: (3 - y, x))),
    "x": ("dp", dp_pairs(lambda y, x: (y, 1 - x))),
    "core": ("mp", mp_pairs(lambda z, h, c: (z, h, 1 - c))),
    "g0": ("mp", mp_pairs(lambda z, h, c: (RING[gray(z) ^ 1], h, c))),
    "g1": ("mp", mp_pairs(lambda z, h, c: (RING[gray(z) ^ 2], h, c))),
    "g2": ("mp", mp_pairs(lambda z, h, c: (RING[gray(z) ^ 4], h, c))),
    "xh": ("mp", mp_pairs(lambda z, h, c: (z, 1 - h, c))),
}

ORDERS = (("y1", "y3", "x"), ("y3", "x", "y1"), ("x", "y1", "y3"))
PIECES = (
    (("out", 0, 8), ("value", 0, 3)),
    (("value", 3, 5), ("query", 0, 5)),
    (("query", 5, 3), ("key", 0, 8)),
)
UNIT = 16


def piece_rows(piece):
    return sum(count for _, _, count in piece) * UNIT


def swap(value, step):
    axis, pairs = PAIRS[step]
    return lax.ppermute(value, axis, pairs)


def position():
    return jnp.stack([lax.axis_index("dp").astype(jnp.int32), lax.axis_index("mp").astype(jnp.int32)])


def piece_code(where, i):
    dp = where[0]
    y, x = dp >> 1, dp & 1
    bit = {"y1": (y ^ (y >> 1)) & 1, "y3": y >> 1, "x": x}
    return bit[ORDERS[i][0]] * 4 + bit[ORDERS[i][1]] * 2


def row_code(where):
    mp = where[1]
    z, c = mp >> 2, mp & 1
    g = z ^ (z >> 1)
    return c * 4 + (g & 1) * 2 + ((g >> 1) & 1)


def mm(a, b, ca, cb):
    return lax.dot_general(a, b, (((ca,), (cb,)), ((), ())), preferred_element_type=F32)


def split(g):
    high = g.astype(BF16)
    low = (g - high.astype(F32)).astype(BF16)
    return high, low


def joined(high, low):
    return high.astype(F32) + low.astype(F32)


def gain_rows(g):
    high, low = split(g)
    width = g.shape[1]
    row = lax.broadcasted_iota(jnp.int32, (EXTRA, width), 0)
    high = jnp.broadcast_to(high.astype(F32), (EXTRA, width))
    low = jnp.broadcast_to(low.astype(F32), (EXTRA, width))
    return jnp.where(row == 0, high, jnp.where(row == 1, low, 0.0)).astype(BF16)


def gain_of(rows):
    rows = rows.astype(F32)
    return rows[0:1] + rows[1:2]


def norm_of(rows):
    rows = rows.astype(F32)
    rstd = lax.rsqrt(jnp.mean(rows * rows, axis=-1, keepdims=True) + 1e-06)
    return rows * rstd, rstd


def whole(count):
    return [pl.BlockSpec(memory_space=pltpu.VMEM)] * count


SCALARS = pl.BlockSpec(memory_space=pltpu.SMEM)


def front_kernel(where, *refs):
    sources, refs = refs[:7], refs[7:]
    outs, refs = refs[:6], refs[6:]
    (gq, gk, gv), refs = refs[:3], refs[3:]
    copied, refs = refs[:7], refs[7:]
    (att, grad_att), refs = refs[:2], refs[2:]
    scratch, sem = dict(zip(("out", "value", "query", "key"), refs[:4])), refs[4]
    copies = [pltpu.make_async_copy(a, b, sem.at[i]) for i, (a, b) in enumerate(zip(sources, copied))]
    for copy in copies:
        copy.start()
    og, wo, q_all, k_all, v_all, x, gain_ref = copied
    copies[0].wait()
    copies[1].wait()
    grad_att[...] = mm(og[...], wo[...], 1, 1).astype(BF16)
    for copy in copies[2:]:
        copy.wait()
    for h in range(q_all.shape[1] // HD):
        col = pl.ds(h * HD, HD)
        q, k, v, ga = q_all[:, col], k_all[:, col], v_all[:, col], grad_att[:, col]
        scores = mm(q, k, 1, 1)
        top = jnp.max(scores, axis=-1, keepdims=True)
        e = jnp.exp(scores - top)
        probs = e * (1.0 / jnp.sum(e, axis=-1, keepdims=True))
        low = probs.astype(BF16)
        att[:, col] = mm(low, v, 1, 0).astype(BF16)
        grad_prob = mm(ga, v, 1, 1)
        delta = jnp.sum(probs * grad_prob, axis=-1, keepdims=True)
        grad_score = (probs * (grad_prob - delta)).astype(BF16)
        gq[:, col] = mm(grad_score, k, 1, 0).astype(BF16)
        gv[col, :] = mm(ga, low, 0, 0).astype(BF16)
        gk[col, :] = mm(q, grad_score, 0, 0).astype(BF16)
    scratch["out"][...] = mm(att[...], og[...], 0, 0).astype(BF16)
    unit, _ = norm_of(x[...])
    normed = (unit * gain_ref[...]).astype(BF16)
    scratch["value"][...] = mm(normed, gv[...], 0, 1).astype(BF16)
    scratch["query"][...] = mm(normed, gq[...], 0, 0).astype(BF16)
    scratch["key"][...] = mm(normed, gk[...], 0, 1).astype(BF16)
    for i, piece in enumerate(PIECES):
        code = piece_code(where, i)
        size = piece_rows(piece)
        for p in range(8):
            dst = outs[2 * i] if p >= 4 else outs[2 * i + 1]
            for at, src, rows in spans(piece, p, p ^ code, size):
                if src == "out":
                    dst[pl.ds(at, 64), :] = scratch[src][rows, :512]
                    dst[pl.ds(at + 64, 64), :] = scratch[src][rows, 512:]
                else:
                    dst[pl.ds(at, rows.size), :] = scratch[src][rows, :]


def spans(piece, p, block, size):
    at = (p % 4) * size
    for name, first, count in piece:
        if name == "out":
            yield at, name, pl.ds(pl.multiple_of(block * 64, 64), 64)
        else:
            yield at, name, pl.ds(pl.multiple_of(block * 128 + first * UNIT, UNIT), count * UNIT)
        at += count * UNIT


def front(where, weight, og, wo, q, k, v, x):
    (length, depth), width = x.shape, q.shape[1]
    shapes = []
    for piece in PIECES:
        shapes += [jax.ShapeDtypeStruct((4 * piece_rows(piece), width), BF16)] * 2
    shapes += [jax.ShapeDtypeStruct((length, width), BF16)] + [jax.ShapeDtypeStruct((width, length), BF16)] * 2
    sources = [pltpu.with_memory_space_constraint(a, pltpu.HBM) for a in (og, wo, q, k, v, x, weight)]
    return pl.pallas_call(
        front_kernel,
        in_specs=[SCALARS, *[pl.BlockSpec(memory_space=pltpu.HBM)] * 7],
        out_specs=whole(9),
        out_shape=shapes,
        scratch_shapes=[
            *[pltpu.VMEM(a.shape, a.dtype) for a in (og, wo, q, k, v, x, weight)],
            *[pltpu.VMEM((length, width), BF16)] * 2,
            pltpu.VMEM((width, depth), BF16),
            *[pltpu.VMEM((depth, width), BF16)] * 3,
            pltpu.SemaphoreType.DMA((7,)),
        ],
        compiler_params=pltpu.CompilerParams(vmem_limit_bytes=40 << 20),
        cost_estimate=pl.CostEstimate(flops=8 << 30, bytes_accessed=16 << 20, transcendentals=1 << 20),
        name="front",
    )(where, *sources)


def total_kernel(where, x_ref, gq_ref, gk_ref, gv_ref, wq_ref, wk_ref, wv_ref, send_ref, keep_ref, gain_ref, low_ref):
    total = mm(gq_ref[...], wq_ref[...], 1, 1)
    total = total + mm(gk_ref[...], wk_ref[...], 0, 1)
    total = total + mm(gv_ref[...], wv_ref[...], 0, 1)
    unit, _ = norm_of(x_ref[...])
    g = jnp.sum(total * unit, axis=0, keepdims=True)
    low_ref[...] = total.astype(BF16)
    for p in range(8):
        block = p ^ row_code(where)
        dst = send_ref if p >= 4 else keep_ref
        dst[pl.ds((p % 4) * 64, 64), :] = low_ref[pl.ds(pl.multiple_of(block * 64, 64), 64), :]
    send_ref[pl.ds(256, EXTRA), :] = gain_rows(g)
    gain_ref[...] = joined(*split(g))


def total_share(where, inputs, gq, gk, gv, wq, wk, wv):
    length, depth = inputs.shape
    half = length // 2
    return pl.pallas_call(
        total_kernel,
        in_specs=[SCALARS, *whole(7)],
        out_specs=whole(3),
        out_shape=[
            jax.ShapeDtypeStruct((half + EXTRA, depth), BF16),
            jax.ShapeDtypeStruct((half, depth), BF16),
            jax.ShapeDtypeStruct((1, depth), F32),
        ],
        scratch_shapes=[pltpu.VMEM((length, depth), BF16)],
        compiler_params=pltpu.CompilerParams(vmem_limit_bytes=20 << 20),
        cost_estimate=pl.CostEstimate(flops=2 << 30, bytes_accessed=8 << 20, transcendentals=0),
        name="total_share",
    )(where, inputs, gq, gk, gv, wq, wk, wv)


def mp_step_kernel(rows, first, ties, gain_ref, *refs):
    *sums, last = refs[: -2 - ties]
    send_ref, out_ref = refs[-2:]
    value = sums[0][pl.ds(first, rows), :].astype(F32)
    for ref in (*sums[1:], last):
        value = value + ref[pl.ds(first, rows), :].astype(F32)
    send_ref[pl.ds(0, rows), :] = value.astype(BF16)
    got = last[pl.ds(last.shape[0] - EXTRA, EXTRA), :]
    g = gain_ref[...] + gain_of(got)
    send_ref[pl.ds(rows, EXTRA), :] = gain_rows(g)
    out_ref[...] = joined(*split(g))


def mp_step(gain, sums, rows, first, ties=()):
    depth = gain.shape[1]
    return pl.pallas_call(
        functools.partial(mp_step_kernel, rows, first, len(ties)),
        in_specs=[*whole(1 + len(sums)), *[ANYWHERE] * len(ties)],
        out_specs=whole(2),
        out_shape=[jax.ShapeDtypeStruct((rows + EXTRA, depth), BF16), jax.ShapeDtypeStruct((1, depth), F32)],
        compiler_params=pltpu.CompilerParams(vmem_limit_bytes=4 << 20),
        cost_estimate=pl.CostEstimate(flops=1 << 10, bytes_accessed=1 << 10, transcendentals=0),
        name="mp_step",
    )(gain, *sums, *ties)


def rows_kernel(where, x_ref, og_ref, weight_ref, gain_ref, mine_ref, got_ref, *refs):
    out_ref, sum_ref = refs[-2:]
    n = out_ref.shape[0]
    gradient = mine_ref[pl.ds(0, n), :].astype(F32) + got_ref[pl.ds(0, n), :].astype(F32)
    unit, rstd = norm_of(x_ref[...])
    scaled = gradient * weight_ref[...]
    inner = jnp.mean(scaled * unit, axis=-1, keepdims=True)
    out_ref[...] = (og_ref[...].astype(F32) + rstd * (scaled - unit * inner)).astype(BF16)
    g = gain_ref[...] + gain_of(got_ref[pl.ds(n, EXTRA), :])
    for j in range(8):
        for i in range(8):
            sum_ref[i, pl.ds(j, 1), :] = g[:, j * 128 : (j + 1) * 128]


def own_rows(where, inputs, og, weight, gain, mine, got, ties):
    n, depth = mine.shape[0] - EXTRA, mine.shape[1]

    def fixed(shape):
        return pl.BlockSpec(shape, lambda i, c: (0, 0))

    row = pl.BlockSpec((n, depth), lambda i, c: (row_code(c), 0))
    return pl.pallas_call(
        rows_kernel,
        grid_spec=pltpu.PrefetchScalarGridSpec(
            num_scalar_prefetch=1,
            grid=(1,),
            in_specs=[row, row, fixed((1, depth)), fixed((1, depth)), fixed(mine.shape), fixed(got.shape), *[ANYWHERE] * len(ties)],
            out_specs=[fixed((n, depth)), pl.BlockSpec((8, 8, 128), lambda i, c: (0, 0, 0))],
        ),
        out_shape=[jax.ShapeDtypeStruct((n, depth), BF16), jax.ShapeDtypeStruct((8, 8, 128), F32)],
        compiler_params=pltpu.CompilerParams(vmem_limit_bytes=4 << 20),
        cost_estimate=pl.CostEstimate(flops=1 << 10, bytes_accessed=1 << 10, transcendentals=0),
        name="own_rows",
    )(where, inputs, og, weight, gain, mine, got, *ties)


ANYWHERE = pl.BlockSpec(memory_space=pl.ANY)


def place_kernel(late, where, *refs):
    halves, sem = refs[:3], refs[-1]
    outs = refs[7:11] if late else refs[3:7]
    if not late:
        refs[7][...] = jnp.zeros(refs[7].shape, F32)
    named = dict(zip(("query", "key", "value", "out"), outs))
    copies = []
    for i, piece in enumerate(PIECES):
        code = piece_code(where, i)
        for p in range(4 * late, 4 * late + 4):
            for at, name, rows in spans(piece, p, p ^ code, piece_rows(piece)):
                if name == "out":
                    pairs = [(at, 64, named[name].at[rows, pl.ds(0, 512)]), (at + 64, 64, named[name].at[rows, pl.ds(512, 512)])]
                else:
                    pairs = [(at, rows.size, named[name].at[rows, :])]
                for first, n, dst in pairs:
                    copy = pltpu.make_async_copy(halves[i].at[pl.ds(first, n), :], dst, sem.at[len(copies)])
                    copy.start()
                    copies.append(copy)
    for copy in copies:
        copy.wait()


def place(late, where, halves, outs, depth, width):
    shapes = [jax.ShapeDtypeStruct((depth, width), BF16)] * 3 + [jax.ShapeDtypeStruct((width, depth), BF16)]
    return pl.pallas_call(
        functools.partial(place_kernel, late),
        in_specs=[SCALARS, *whole(3), *[ANYWHERE] * len(outs)],
        out_specs=[ANYWHERE] * 4 + whole(1 - late),
        out_shape=shapes + [jax.ShapeDtypeStruct((8, 128), F32)] * (1 - late),
        scratch_shapes=[pltpu.SemaphoreType.DMA((28,))],
        input_output_aliases={4 + i: i for i in range(len(outs))},
        compiler_params=pltpu.CompilerParams(vmem_limit_bytes=4 << 20),
        cost_estimate=pl.CostEstimate(flops=(1 << 36) if late else (1 << 10), bytes_accessed=1 << 10, transcendentals=0),
        name="place_late" if late else "place_early",
    )(where, *halves, *outs)


def place_rows_kernel(where, low_ref, high_ref, out_ref, sem):
    code = row_code(where)
    copies = []
    for p in range(8):
        src = high_ref if p >= 4 else low_ref
        rows = pl.ds(pl.multiple_of((p ^ code) * 64, 64), 64)
        copy = pltpu.make_async_copy(src.at[pl.ds((p % 4) * 64, 64), :], out_ref.at[rows, :], sem.at[p])
        copy.start()
        copies.append(copy)
    for copy in copies:
        copy.wait()


def place_rows(where, low, high):
    return pl.pallas_call(
        place_rows_kernel,
        in_specs=[SCALARS, *whole(2)],
        out_specs=ANYWHERE,
        out_shape=jax.ShapeDtypeStruct((2 * low.shape[0], low.shape[1]), BF16),
        scratch_shapes=[pltpu.SemaphoreType.DMA((8,))],
        compiler_params=pltpu.CompilerParams(vmem_limit_bytes=4 << 20),
        cost_estimate=pl.CostEstimate(flops=1 << 10, bytes_accessed=2 << 20, transcendentals=0),
        name="place_rows",
    )(where, low, high)


def plus(*values):
    total = values[0].astype(F32)
    for value in values[1:]:
        total = total + value.astype(F32)
    return total.astype(BF16)


def after(value, first):
    return lax.optimization_barrier((value, *first))[0]


def shards(
    inputs,
    norm_gain_vector,
    query_saved,
    key_saved,
    value_saved,
    w_query,
    w_key,
    w_value,
    w_out,
    output_gradient,
):
    length, depth = inputs.shape
    width = query_saved.shape[1]
    where = position()
    weight = norm_gain_vector.reshape(1, depth)
    *pieces, gq, gk, gv = front(where, weight, output_gradient, w_out, query_saved, key_saved, value_saved, inputs)
    m_send, m_keep, gain = total_share(where, inputs, gq, gk, gv, w_query, w_key, w_value)

    sends, keeps = pieces[0::2], pieces[1::2]
    sizes = [piece_rows(piece) for piece in PIECES]
    first = [swap(s, o[0]) for s, o in zip(sends, ORDERS)]
    r1 = swap(m_send, "core")
    send, gain = mp_step(gain, (m_keep, r1), 128, 128)
    r2 = swap(send, "g0")
    second = [plus(k[2 * n :], r[2 * n :]) for k, r, n in zip(keeps, first, sizes)]
    send, gain = mp_step(gain, (m_keep, r1, r2), 64, 64, second)
    second = [swap(v, o[1]) for v, o in zip(second, ORDERS)]
    r3 = swap(send, "g1")
    mine = [plus(k[: 2 * n], r[: 2 * n], s) for k, r, s, n in zip(keeps, first, second, sizes)]
    third = [swap(v, o[2]) for v, o in zip(mine, ORDERS)]
    send, gain = mp_step(gain, (m_keep, r1, r2, r3), 64, 0, mine)
    r4 = swap(send, "g2")
    quarter = [plus(v, t) for v, t in zip(mine, third)]
    back = [swap(v, o[1]) for v, o in zip(quarter, ORDERS)]
    half = [jnp.concatenate([v, b]) for v, b in zip(quarter, back)]
    last = [swap(v, o[0]) for v, o in zip(half, ORDERS)]
    send, gain = mp_step(gain, (send, r4), 64, 0, quarter)
    r5 = swap(send, "xh")
    rows, gains = own_rows(where, inputs, output_gradient, weight, gain, send, r5, half)
    *outs, placed = place(0, where, half, (), depth, width)
    for step in ("g1", "g0"):
        rows = jnp.concatenate([rows, swap(rows, step)])
    gains = lax.all_to_all(gains, "dp", 0, 0)
    rows = after(rows, last)
    grad_inputs = place_rows(where, rows, swap(rows, "core"))
    outs = place(1, where, last, outs, depth, width)
    return (grad_inputs, *outs, jnp.sum(gains, axis=0).reshape(depth))


def solution(mesh):
    return jax.shard_map(
        shards,
        mesh=mesh,
        in_specs=(
            P("dp", None),
            P(),
            P("dp", "mp"),
            P("dp", "mp"),
            P("dp", "mp"),
            P(None, "mp"),
            P(None, "mp"),
            P(None, "mp"),
            P("mp", None),
            P("dp", None),
        ),
        out_specs=(P("dp", None), P(None, "mp"), P(None, "mp"), P(None, "mp"), P("mp", None), P()),
        check_vma=False,
    )
```

```python
import functools

import jax
import jax.numpy as jnp
from jax import lax
from jax.experimental import pallas as pl
from jax.experimental.pallas import tpu as pltpu
from jax.sharding import PartitionSpec as P

HD = 128
F32 = jnp.float32
BF16 = jnp.bfloat16
EXTRA = 16


def gray(z):
    return z ^ (z >> 1)


RING = {gray(z): z for z in range(8)}


def dp_pairs(flip):
    return [(y * 2 + x, (lambda t: t[0] * 2 + t[1])(flip(y, x))) for y in range(4) for x in range(2)]


def mp_pairs(flip):
    return [
        (z * 4 + h * 2 + c, (lambda t: t[0] * 4 + t[1] * 2 + t[2])(flip(z, h, c)))
        for z in range(8)
        for h in range(2)
        for c in range(2)
    ]


PAIRS = {
    "y1": ("dp", dp_pairs(lambda y, x: (y ^ 1, x))),
    "y3": ("dp", dp_pairs(lambda y, x: (3 - y, x))),
    "x": ("dp", dp_pairs(lambda y, x: (y, 1 - x))),
    "core": ("mp", mp_pairs(lambda z, h, c: (z, h, 1 - c))),
    "g0": ("mp", mp_pairs(lambda z, h, c: (RING[gray(z) ^ 1], h, c))),
    "g1": ("mp", mp_pairs(lambda z, h, c: (RING[gray(z) ^ 2], h, c))),
    "g2": ("mp", mp_pairs(lambda z, h, c: (RING[gray(z) ^ 4], h, c))),
    "xh": ("mp", mp_pairs(lambda z, h, c: (z, 1 - h, c))),
}

ORDERS = (("y1", "y3", "x"), ("y3", "x", "y1"), ("x", "y1", "y3"))
PIECES = (
    (("out", 0, 8), ("value", 0, 3)),
    (("value", 3, 5), ("query", 0, 5)),
    (("query", 5, 3), ("key", 0, 8)),
)
UNIT = 16


def piece_rows(piece):
    return sum(count for _, _, count in piece) * UNIT


def swap(value, step):
    axis, pairs = PAIRS[step]
    return lax.ppermute(value, axis, pairs)


def position():
    return jnp.stack([lax.axis_index("dp").astype(jnp.int32), lax.axis_index("mp").astype(jnp.int32)])


def piece_code(where, i):
    dp = where[0]
    y, x = dp >> 1, dp & 1
    bit = {"y1": (y ^ (y >> 1)) & 1, "y3": y >> 1, "x": x}
    return bit[ORDERS[i][0]] * 4 + bit[ORDERS[i][1]] * 2


def row_code(where):
    mp = where[1]
    z, c = mp >> 2, mp & 1
    g = z ^ (z >> 1)
    return c * 4 + (g & 1) * 2 + ((g >> 1) & 1)


def mm(a, b, ca, cb):
    return lax.dot_general(a, b, (((ca,), (cb,)), ((), ())), preferred_element_type=F32)


def split(g):
    high = g.astype(BF16)
    low = (g - high.astype(F32)).astype(BF16)
    return high, low


def joined(high, low):
    return high.astype(F32) + low.astype(F32)


def gain_rows(g):
    high, low = split(g)
    width = g.shape[1]
    row = lax.broadcasted_iota(jnp.int32, (EXTRA, width), 0)
    high = jnp.broadcast_to(high.astype(F32), (EXTRA, width))
    low = jnp.broadcast_to(low.astype(F32), (EXTRA, width))
    return jnp.where(row == 0, high, jnp.where(row == 1, low, 0.0)).astype(BF16)


def gain_of(rows):
    rows = rows.astype(F32)
    return rows[0:1] + rows[1:2]


def norm_of(rows):
    rows = rows.astype(F32)
    rstd = lax.rsqrt(jnp.mean(rows * rows, axis=-1, keepdims=True) + 1e-06)
    return rows * rstd, rstd


def whole(count):
    return [pl.BlockSpec(memory_space=pltpu.VMEM)] * count


SCALARS = pl.BlockSpec(memory_space=pltpu.SMEM)


def front_kernel(where, *refs):
    sources, refs = refs[:7], refs[7:]
    outs, refs = refs[:6], refs[6:]
    (gq, gk, gv), refs = refs[:3], refs[3:]
    copied, refs = refs[:7], refs[7:]
    (att, grad_att), refs = refs[:2], refs[2:]
    scratch, sem = dict(zip(("out", "value", "query", "key"), refs[:4])), refs[4]
    copies = [pltpu.make_async_copy(a, b, sem.at[i]) for i, (a, b) in enumerate(zip(sources, copied))]
    for copy in copies:
        copy.start()
    og, wo, q_all, k_all, v_all, x, gain_ref = copied
    copies[0].wait()
    copies[1].wait()
    grad_att[...] = mm(og[...], wo[...], 1, 1).astype(BF16)
    for copy in copies[2:]:
        copy.wait()
    for h in range(q_all.shape[1] // HD):
        col = pl.ds(h * HD, HD)
        q, k, v, ga = q_all[:, col], k_all[:, col], v_all[:, col], grad_att[:, col]
        scores = mm(q, k, 1, 1)
        top = jnp.max(scores, axis=-1, keepdims=True)
        e = jnp.exp(scores - top)
        probs = e * (1.0 / jnp.sum(e, axis=-1, keepdims=True))
        low = probs.astype(BF16)
        att[:, col] = mm(low, v, 1, 0).astype(BF16)
        grad_prob = mm(ga, v, 1, 1)
        delta = jnp.sum(probs * grad_prob, axis=-1, keepdims=True)
        grad_score = (probs * (grad_prob - delta)).astype(BF16)
        gq[:, col] = mm(grad_score, k, 1, 0).astype(BF16)
        gv[col, :] = mm(ga, low, 0, 0).astype(BF16)
        gk[col, :] = mm(q, grad_score, 0, 0).astype(BF16)
    scratch["out"][...] = mm(att[...], og[...], 0, 0).astype(BF16)
    unit, _ = norm_of(x[...])
    normed = (unit * gain_ref[...]).astype(BF16)
    scratch["value"][...] = mm(normed, gv[...], 0, 1).astype(BF16)
    scratch["query"][...] = mm(normed, gq[...], 0, 0).astype(BF16)
    scratch["key"][...] = mm(normed, gk[...], 0, 1).astype(BF16)
    for i, piece in enumerate(PIECES):
        code = piece_code(where, i)
        size = piece_rows(piece)
        for p in range(8):
            dst = outs[2 * i] if p >= 4 else outs[2 * i + 1]
            for at, src, rows in spans(piece, p, p ^ code, size):
                if src == "out":
                    dst[pl.ds(at, 64), :] = scratch[src][rows, :512]
                    dst[pl.ds(at + 64, 64), :] = scratch[src][rows, 512:]
                else:
                    dst[pl.ds(at, rows.size), :] = scratch[src][rows, :]


def spans(piece, p, block, size):
    at = (p % 4) * size
    for name, first, count in piece:
        if name == "out":
            yield at, name, pl.ds(pl.multiple_of(block * 64, 64), 64)
        else:
            yield at, name, pl.ds(pl.multiple_of(block * 128 + first * UNIT, UNIT), count * UNIT)
        at += count * UNIT


def front(where, weight, og, wo, q, k, v, x):
    (length, depth), width = x.shape, q.shape[1]
    shapes = []
    for piece in PIECES:
        shapes += [jax.ShapeDtypeStruct((4 * piece_rows(piece), width), BF16)] * 2
    shapes += [jax.ShapeDtypeStruct((length, width), BF16)] + [jax.ShapeDtypeStruct((width, length), BF16)] * 2
    sources = [pltpu.with_memory_space_constraint(a, pltpu.HBM) for a in (og, wo, q, k, v, x, weight)]
    return pl.pallas_call(
        front_kernel,
        in_specs=[SCALARS, *[pl.BlockSpec(memory_space=pltpu.HBM)] * 7],
        out_specs=whole(9),
        out_shape=shapes,
        scratch_shapes=[
            *[pltpu.VMEM(a.shape, a.dtype) for a in (og, wo, q, k, v, x, weight)],
            *[pltpu.VMEM((length, width), BF16)] * 2,
            pltpu.VMEM((width, depth), BF16),
            *[pltpu.VMEM((depth, width), BF16)] * 3,
            pltpu.SemaphoreType.DMA((7,)),
        ],
        compiler_params=pltpu.CompilerParams(vmem_limit_bytes=40 << 20),
        cost_estimate=pl.CostEstimate(flops=8 << 30, bytes_accessed=16 << 20, transcendentals=1 << 20),
        name="front",
    )(where, *sources)


def total_kernel(where, x_ref, gq_ref, gk_ref, gv_ref, wq_ref, wk_ref, wv_ref, send_ref, keep_ref, gain_ref, low_ref):
    total = mm(gq_ref[...], wq_ref[...], 1, 1)
    total = total + mm(gk_ref[...], wk_ref[...], 0, 1)
    total = total + mm(gv_ref[...], wv_ref[...], 0, 1)
    unit, _ = norm_of(x_ref[...])
    g = jnp.sum(total * unit, axis=0, keepdims=True)
    low_ref[...] = total.astype(BF16)
    for p in range(8):
        block = p ^ row_code(where)
        dst = send_ref if p >= 4 else keep_ref
        dst[pl.ds((p % 4) * 64, 64), :] = low_ref[pl.ds(pl.multiple_of(block * 64, 64), 64), :]
    send_ref[pl.ds(256, EXTRA), :] = gain_rows(g)
    gain_ref[...] = joined(*split(g))


def total_share(where, inputs, gq, gk, gv, wq, wk, wv):
    length, depth = inputs.shape
    half = length // 2
    return pl.pallas_call(
        total_kernel,
        in_specs=[SCALARS, *whole(7)],
        out_specs=whole(3),
        out_shape=[
            jax.ShapeDtypeStruct((half + EXTRA, depth), BF16),
            jax.ShapeDtypeStruct((half, depth), BF16),
            jax.ShapeDtypeStruct((1, depth), F32),
        ],
        scratch_shapes=[pltpu.VMEM((length, depth), BF16)],
        compiler_params=pltpu.CompilerParams(vmem_limit_bytes=20 << 20),
        cost_estimate=pl.CostEstimate(flops=2 << 30, bytes_accessed=8 << 20, transcendentals=0),
        name="total_share",
    )(where, inputs, gq, gk, gv, wq, wk, wv)


def mp_step_kernel(rows, first, ties, gain_ref, *refs):
    *sums, last = refs[: -2 - ties]
    send_ref, out_ref = refs[-2:]
    value = sums[0][pl.ds(first, rows), :].astype(F32)
    for ref in (*sums[1:], last):
        value = value + ref[pl.ds(first, rows), :].astype(F32)
    send_ref[pl.ds(0, rows), :] = value.astype(BF16)
    got = last[pl.ds(last.shape[0] - EXTRA, EXTRA), :]
    g = gain_ref[...] + gain_of(got)
    send_ref[pl.ds(rows, EXTRA), :] = gain_rows(g)
    out_ref[...] = joined(*split(g))


def mp_step(gain, sums, rows, first, ties=()):
    depth = gain.shape[1]
    return pl.pallas_call(
        functools.partial(mp_step_kernel, rows, first, len(ties)),
        in_specs=[*whole(1 + len(sums)), *[ANYWHERE] * len(ties)],
        out_specs=whole(2),
        out_shape=[jax.ShapeDtypeStruct((rows + EXTRA, depth), BF16), jax.ShapeDtypeStruct((1, depth), F32)],
        compiler_params=pltpu.CompilerParams(vmem_limit_bytes=4 << 20),
        cost_estimate=pl.CostEstimate(flops=1 << 10, bytes_accessed=1 << 10, transcendentals=0),
        name="mp_step",
    )(gain, *sums, *ties)


def rows_kernel(where, x_ref, og_ref, weight_ref, gain_ref, mine_ref, got_ref, *refs):
    out_ref, sum_ref = refs[-2:]
    n = out_ref.shape[0]
    gradient = mine_ref[pl.ds(0, n), :].astype(F32) + got_ref[pl.ds(0, n), :].astype(F32)
    unit, rstd = norm_of(x_ref[...])
    scaled = gradient * weight_ref[...]
    inner = jnp.mean(scaled * unit, axis=-1, keepdims=True)
    out_ref[...] = (og_ref[...].astype(F32) + rstd * (scaled - unit * inner)).astype(BF16)
    g = gain_ref[...] + gain_of(got_ref[pl.ds(n, EXTRA), :])
    for j in range(8):
        for i in range(8):
            sum_ref[i, pl.ds(j, 1), :] = g[:, j * 128 : (j + 1) * 128]


def own_rows(where, inputs, og, weight, gain, mine, got, ties):
    n, depth = mine.shape[0] - EXTRA, mine.shape[1]

    def fixed(shape):
        return pl.BlockSpec(shape, lambda i, c: (0, 0))

    row = pl.BlockSpec((n, depth), lambda i, c: (row_code(c), 0))
    return pl.pallas_call(
        rows_kernel,
        grid_spec=pltpu.PrefetchScalarGridSpec(
            num_scalar_prefetch=1,
            grid=(1,),
            in_specs=[row, row, fixed((1, depth)), fixed((1, depth)), fixed(mine.shape), fixed(got.shape), *[ANYWHERE] * len(ties)],
            out_specs=[fixed((n, depth)), pl.BlockSpec((8, 8, 128), lambda i, c: (0, 0, 0))],
        ),
        out_shape=[jax.ShapeDtypeStruct((n, depth), BF16), jax.ShapeDtypeStruct((8, 8, 128), F32)],
        compiler_params=pltpu.CompilerParams(vmem_limit_bytes=4 << 20),
        cost_estimate=pl.CostEstimate(flops=1 << 10, bytes_accessed=1 << 10, transcendentals=0),
        name="own_rows",
    )(where, inputs, og, weight, gain, mine, got, *ties)


ANYWHERE = pl.BlockSpec(memory_space=pl.ANY)


def place_kernel(late, where, *refs):
    halves, sem = refs[:3], refs[-1]
    outs = refs[7:11] if late else refs[3:7]
    if not late:
        refs[7][...] = jnp.zeros(refs[7].shape, F32)
    named = dict(zip(("query", "key", "value", "out"), outs))
    copies = []
    for i, piece in enumerate(PIECES):
        code = piece_code(where, i)
        for p in range(4 * late, 4 * late + 4):
            for at, name, rows in spans(piece, p, p ^ code, piece_rows(piece)):
                if name == "out":
                    pairs = [(at, 64, named[name].at[rows, pl.ds(0, 512)]), (at + 64, 64, named[name].at[rows, pl.ds(512, 512)])]
                else:
                    pairs = [(at, rows.size, named[name].at[rows, :])]
                for first, n, dst in pairs:
                    copy = pltpu.make_async_copy(halves[i].at[pl.ds(first, n), :], dst, sem.at[len(copies)])
                    copy.start()
                    copies.append(copy)
    for copy in copies:
        copy.wait()


def place(late, where, halves, outs, depth, width):
    shapes = [jax.ShapeDtypeStruct((depth, width), BF16)] * 3 + [jax.ShapeDtypeStruct((width, depth), BF16)]
    return pl.pallas_call(
        functools.partial(place_kernel, late),
        in_specs=[SCALARS, *whole(3), *[ANYWHERE] * len(outs)],
        out_specs=[ANYWHERE] * 4 + whole(1 - late),
        out_shape=shapes + [jax.ShapeDtypeStruct((8, 128), F32)] * (1 - late),
        scratch_shapes=[pltpu.SemaphoreType.DMA((28,))],
        input_output_aliases={4 + i: i for i in range(len(outs))},
        compiler_params=pltpu.CompilerParams(vmem_limit_bytes=4 << 20),
        cost_estimate=pl.CostEstimate(flops=(1 << 36) if late else (1 << 10), bytes_accessed=1 << 10, transcendentals=0),
        name="place_late" if late else "place_early",
    )(where, *halves, *outs)


def place_rows_kernel(where, low_ref, high_ref, out_ref, sem):
    code = row_code(where)
    copies = []
    for p in range(8):
        src = high_ref if p >= 4 else low_ref
        rows = pl.ds(pl.multiple_of((p ^ code) * 64, 64), 64)
        copy = pltpu.make_async_copy(src.at[pl.ds((p % 4) * 64, 64), :], out_ref.at[rows, :], sem.at[p])
        copy.start()
        copies.append(copy)
    for copy in copies:
        copy.wait()


def place_rows(where, low, high):
    return pl.pallas_call(
        place_rows_kernel,
        in_specs=[SCALARS, *whole(2)],
        out_specs=ANYWHERE,
        out_shape=jax.ShapeDtypeStruct((2 * low.shape[0], low.shape[1]), BF16),
        scratch_shapes=[pltpu.SemaphoreType.DMA((8,))],
        compiler_params=pltpu.CompilerParams(vmem_limit_bytes=4 << 20),
        cost_estimate=pl.CostEstimate(flops=1 << 10, bytes_accessed=2 << 20, transcendentals=0),
        name="place_rows",
    )(where, low, high)


def plus(*values):
    total = values[0].astype(F32)
    for value in values[1:]:
        total = total + value.astype(F32)
    return total.astype(BF16)


def after(value, first):
    return lax.optimization_barrier((value, *first))[0]


def shards(
    inputs,
    norm_gain_vector,
    query_saved,
    key_saved,
    value_saved,
    w_query,
    w_key,
    w_value,
    w_out,
    output_gradient,
):
    length, depth = inputs.shape
    width = query_saved.shape[1]
    where = position()
    weight = norm_gain_vector.reshape(1, depth)
    *pieces, gq, gk, gv = front(where, weight, output_gradient, w_out, query_saved, key_saved, value_saved, inputs)
    m_send, m_keep, gain = total_share(where, inputs, gq, gk, gv, w_query, w_key, w_value)

    sends, keeps = pieces[0::2], pieces[1::2]
    sizes = [piece_rows(piece) for piece in PIECES]
    first = [swap(s, o[0]) for s, o in zip(sends, ORDERS)]
    r1 = swap(m_send, "core")
    send, gain = mp_step(gain, (m_keep, r1), 128, 128)
    r2 = swap(send, "g0")
    send, gain = mp_step(gain, (m_keep, r1, r2), 64, 64)
    second = [after(plus(k[2 * n :], r[2 * n :]), [send]) for k, r, n in zip(keeps, first, sizes)]
    r3 = swap(send, "g1")
    received = [swap(v, o[1]) for v, o in zip(second, ORDERS)]
    send, gain = mp_step(gain, (m_keep, r1, r2, r3), 64, 0, second)
    r4 = swap(send, "g2")
    mine = [plus(k[: 2 * n], r[: 2 * n], s) for k, r, s, n in zip(keeps, first, received, sizes)]
    third = [swap(v, o[2]) for v, o in zip(mine, ORDERS)]
    send, gain = mp_step(gain, (send, r4), 64, 0, mine)
    r5 = swap(send, "xh")
    quarter = [after(plus(v, t), [send]) for v, t in zip(mine, third)]
    back = [swap(v, o[1]) for v, o in zip(quarter, ORDERS)]
    half = [jnp.concatenate([v, b]) for v, b in zip(quarter, back)]
    last = [swap(v, o[0]) for v, o in zip(half, ORDERS)]
    rows, gains = own_rows(where, inputs, output_gradient, weight, gain, send, r5, quarter)
    *outs, placed = place(0, where, half, (), depth, width)
    got = swap(rows, "g1")
    rows = jnp.concatenate([after(rows, half), got])
    rows = jnp.concatenate([rows, swap(rows, "g0")])
    gains = lax.all_to_all(after(gains, half), "dp", 0, 0)
    rows = after(rows, last)
    grad_inputs = place_rows(where, rows, swap(rows, "core"))
    outs = place(1, where, last, outs, depth, width)
    return (grad_inputs, *outs, jnp.sum(gains, axis=0).reshape(depth))


def solution(mesh):
    return jax.shard_map(
        shards,
        mesh=mesh,
        in_specs=(
            P("dp", None),
            P(),
            P("dp", "mp"),
            P("dp", "mp"),
            P("dp", "mp"),
            P(None, "mp"),
            P(None, "mp"),
            P(None, "mp"),
            P("mp", None),
            P("dp", None),
        ),
        out_specs=(P("dp", None), P(None, "mp"), P(None, "mp"), P(None, "mp"), P("mp", None), P()),
        check_vma=False,
    )
```

```python
import functools

import jax
import jax.numpy as jnp
from jax import lax
from jax.experimental import pallas as pl
from jax.experimental.pallas import tpu as pltpu
from jax.sharding import PartitionSpec as P

HD = 128
F32 = jnp.float32
BF16 = jnp.bfloat16
EXTRA = 16


def gray(z):
    return z ^ (z >> 1)


RING = {gray(z): z for z in range(8)}


def dp_pairs(flip):
    return [(y * 2 + x, (lambda t: t[0] * 2 + t[1])(flip(y, x))) for y in range(4) for x in range(2)]


def mp_pairs(flip):
    return [
        (z * 4 + h * 2 + c, (lambda t: t[0] * 4 + t[1] * 2 + t[2])(flip(z, h, c)))
        for z in range(8)
        for h in range(2)
        for c in range(2)
    ]


PAIRS = {
    "y1": ("dp", dp_pairs(lambda y, x: (y ^ 1, x))),
    "y3": ("dp", dp_pairs(lambda y, x: (3 - y, x))),
    "x": ("dp", dp_pairs(lambda y, x: (y, 1 - x))),
    "core": ("mp", mp_pairs(lambda z, h, c: (z, h, 1 - c))),
    "g0": ("mp", mp_pairs(lambda z, h, c: (RING[gray(z) ^ 1], h, c))),
    "g1": ("mp", mp_pairs(lambda z, h, c: (RING[gray(z) ^ 2], h, c))),
    "g2": ("mp", mp_pairs(lambda z, h, c: (RING[gray(z) ^ 4], h, c))),
    "xh": ("mp", mp_pairs(lambda z, h, c: (z, 1 - h, c))),
}

ORDERS = (("y1", "y3", "x"), ("y3", "x", "y1"), ("x", "y1", "y3"))
PIECES = (
    (("out", 0, 8), ("value", 0, 3)),
    (("value", 3, 5), ("query", 0, 5)),
    (("query", 5, 3), ("key", 0, 8)),
)
UNIT = 16


def piece_rows(piece):
    return sum(count for _, _, count in piece) * UNIT


def swap(value, step):
    axis, pairs = PAIRS[step]
    return lax.ppermute(value, axis, pairs)


def position():
    return jnp.stack([lax.axis_index("dp").astype(jnp.int32), lax.axis_index("mp").astype(jnp.int32)])


def piece_code(where, i):
    dp = where[0]
    y, x = dp >> 1, dp & 1
    bit = {"y1": (y ^ (y >> 1)) & 1, "y3": y >> 1, "x": x}
    return bit[ORDERS[i][0]] * 4 + bit[ORDERS[i][1]] * 2


def row_code(where):
    mp = where[1]
    z, c = mp >> 2, mp & 1
    g = z ^ (z >> 1)
    return c * 4 + (g & 1) * 2 + ((g >> 1) & 1)


def mm(a, b, ca, cb):
    return lax.dot_general(a, b, (((ca,), (cb,)), ((), ())), preferred_element_type=F32)


def split(g):
    high = g.astype(BF16)
    low = (g - high.astype(F32)).astype(BF16)
    return high, low


def joined(high, low):
    return high.astype(F32) + low.astype(F32)


def gain_rows(g):
    high, low = split(g)
    width = g.shape[1]
    row = lax.broadcasted_iota(jnp.int32, (EXTRA, width), 0)
    high = jnp.broadcast_to(high.astype(F32), (EXTRA, width))
    low = jnp.broadcast_to(low.astype(F32), (EXTRA, width))
    return jnp.where(row == 0, high, jnp.where(row == 1, low, 0.0)).astype(BF16)


def gain_of(rows):
    rows = rows.astype(F32)
    return rows[0:1] + rows[1:2]


def norm_of(rows):
    rows = rows.astype(F32)
    rstd = lax.rsqrt(jnp.mean(rows * rows, axis=-1, keepdims=True) + 1e-06)
    return rows * rstd, rstd


def whole(count):
    return [pl.BlockSpec(memory_space=pltpu.VMEM)] * count


SCALARS = pl.BlockSpec(memory_space=pltpu.SMEM)


def front_kernel(where, *refs):
    sources, refs = refs[:7], refs[7:]
    outs, refs = refs[:6], refs[6:]
    (gq, gk, gv), refs = refs[:3], refs[3:]
    copied, refs = refs[:7], refs[7:]
    (att, grad_att), refs = refs[:2], refs[2:]
    scratch, sem = dict(zip(("out", "value", "query", "key"), refs[:4])), refs[4]
    copies = [pltpu.make_async_copy(a, b, sem.at[i]) for i, (a, b) in enumerate(zip(sources, copied))]
    for copy in copies:
        copy.start()
    og, wo, q_all, k_all, v_all, x, gain_ref = copied
    copies[0].wait()
    copies[1].wait()
    grad_att[...] = mm(og[...], wo[...], 1, 1).astype(BF16)
    for copy in copies[2:]:
        copy.wait()
    for h in range(q_all.shape[1] // HD):
        col = pl.ds(h * HD, HD)
        q, k, v, ga = q_all[:, col], k_all[:, col], v_all[:, col], grad_att[:, col]
        scores = mm(q, k, 1, 1)
        top = jnp.max(scores, axis=-1, keepdims=True)
        e = jnp.exp(scores - top)
        probs = e * (1.0 / jnp.sum(e, axis=-1, keepdims=True))
        low = probs.astype(BF16)
        att[:, col] = mm(low, v, 1, 0).astype(BF16)
        grad_prob = mm(ga, v, 1, 1)
        delta = jnp.sum(probs * grad_prob, axis=-1, keepdims=True)
        grad_score = (probs * (grad_prob - delta)).astype(BF16)
        gq[:, col] = mm(grad_score, k, 1, 0).astype(BF16)
        gv[col, :] = mm(ga, low, 0, 0).astype(BF16)
        gk[col, :] = mm(q, grad_score, 0, 0).astype(BF16)
    scratch["out"][...] = mm(att[...], og[...], 0, 0).astype(BF16)
    unit, _ = norm_of(x[...])
    normed = (unit * gain_ref[...]).astype(BF16)
    scratch["value"][...] = mm(normed, gv[...], 0, 1).astype(BF16)
    scratch["query"][...] = mm(normed, gq[...], 0, 0).astype(BF16)
    scratch["key"][...] = mm(normed, gk[...], 0, 1).astype(BF16)
    for i, piece in enumerate(PIECES):
        code = piece_code(where, i)
        size = piece_rows(piece)
        for p in range(8):
            dst = outs[2 * i] if p >= 4 else outs[2 * i + 1]
            for at, src, rows in spans(piece, p, p ^ code, size):
                if src == "out":
                    dst[pl.ds(at, 64), :] = scratch[src][rows, :512]
                    dst[pl.ds(at + 64, 64), :] = scratch[src][rows, 512:]
                else:
                    dst[pl.ds(at, rows.size), :] = scratch[src][rows, :]


def spans(piece, p, block, size):
    at = (p % 4) * size
    for name, first, count in piece:
        if name == "out":
            yield at, name, pl.ds(pl.multiple_of(block * 64, 64), 64)
        else:
            yield at, name, pl.ds(pl.multiple_of(block * 128 + first * UNIT, UNIT), count * UNIT)
        at += count * UNIT


def front(where, weight, og, wo, q, k, v, x):
    (length, depth), width = x.shape, q.shape[1]
    shapes = []
    for piece in PIECES:
        shapes += [jax.ShapeDtypeStruct((4 * piece_rows(piece), width), BF16)] * 2
    shapes += [jax.ShapeDtypeStruct((length, width), BF16)] + [jax.ShapeDtypeStruct((width, length), BF16)] * 2
    sources = [pltpu.with_memory_space_constraint(a, pltpu.HBM) for a in (og, wo, q, k, v, x, weight)]
    return pl.pallas_call(
        front_kernel,
        in_specs=[SCALARS, *[pl.BlockSpec(memory_space=pltpu.HBM)] * 7],
        out_specs=whole(9),
        out_shape=shapes,
        scratch_shapes=[
            *[pltpu.VMEM(a.shape, a.dtype) for a in (og, wo, q, k, v, x, weight)],
            *[pltpu.VMEM((length, width), BF16)] * 2,
            pltpu.VMEM((width, depth), BF16),
            *[pltpu.VMEM((depth, width), BF16)] * 3,
            pltpu.SemaphoreType.DMA((7,)),
        ],
        compiler_params=pltpu.CompilerParams(vmem_limit_bytes=40 << 20),
        cost_estimate=pl.CostEstimate(flops=8 << 30, bytes_accessed=16 << 20, transcendentals=1 << 20),
        name="front",
    )(where, *sources)


def total_kernel(where, x_ref, gq_ref, gk_ref, gv_ref, wq_ref, wk_ref, wv_ref, send_ref, keep_ref, gain_ref, low_ref):
    total = mm(gq_ref[...], wq_ref[...], 1, 1)
    total = total + mm(gk_ref[...], wk_ref[...], 0, 1)
    total = total + mm(gv_ref[...], wv_ref[...], 0, 1)
    unit, _ = norm_of(x_ref[...])
    g = jnp.sum(total * unit, axis=0, keepdims=True)
    low_ref[...] = total.astype(BF16)
    for p in range(8):
        block = p ^ row_code(where)
        dst = send_ref if p >= 4 else keep_ref
        dst[pl.ds((p % 4) * 64, 64), :] = low_ref[pl.ds(pl.multiple_of(block * 64, 64), 64), :]
    send_ref[pl.ds(256, EXTRA), :] = gain_rows(g)
    gain_ref[...] = joined(*split(g))


def total_share(where, inputs, gq, gk, gv, wq, wk, wv):
    length, depth = inputs.shape
    half = length // 2
    return pl.pallas_call(
        total_kernel,
        in_specs=[SCALARS, *whole(7)],
        out_specs=whole(3),
        out_shape=[
            jax.ShapeDtypeStruct((half + EXTRA, depth), BF16),
            jax.ShapeDtypeStruct((half, depth), BF16),
            jax.ShapeDtypeStruct((1, depth), F32),
        ],
        scratch_shapes=[pltpu.VMEM((length, depth), BF16)],
        compiler_params=pltpu.CompilerParams(vmem_limit_bytes=20 << 20),
        cost_estimate=pl.CostEstimate(flops=2 << 30, bytes_accessed=8 << 20, transcendentals=0),
        name="total_share",
    )(where, inputs, gq, gk, gv, wq, wk, wv)


def mp_step_kernel(rows, first, ties, gain_ref, *refs):
    *sums, last = refs[: -2 - ties]
    send_ref, out_ref = refs[-2:]
    value = sums[0][pl.ds(first, rows), :].astype(F32)
    for ref in (*sums[1:], last):
        value = value + ref[pl.ds(first, rows), :].astype(F32)
    send_ref[pl.ds(0, rows), :] = value.astype(BF16)
    got = last[pl.ds(last.shape[0] - EXTRA, EXTRA), :]
    g = gain_ref[...] + gain_of(got)
    send_ref[pl.ds(rows, EXTRA), :] = gain_rows(g)
    out_ref[...] = joined(*split(g))


def mp_step(gain, sums, rows, first, ties=()):
    depth = gain.shape[1]
    return pl.pallas_call(
        functools.partial(mp_step_kernel, rows, first, len(ties)),
        in_specs=[*whole(1 + len(sums)), *[ANYWHERE] * len(ties)],
        out_specs=whole(2),
        out_shape=[jax.ShapeDtypeStruct((rows + EXTRA, depth), BF16), jax.ShapeDtypeStruct((1, depth), F32)],
        compiler_params=pltpu.CompilerParams(vmem_limit_bytes=4 << 20),
        cost_estimate=pl.CostEstimate(flops=1 << 10, bytes_accessed=1 << 10, transcendentals=0),
        name="mp_step",
    )(gain, *sums, *ties)


def rows_kernel(where, x_ref, og_ref, weight_ref, gain_ref, mine_ref, got_ref, *refs):
    out_ref, sum_ref = refs[-2:]
    n = out_ref.shape[0]
    gradient = mine_ref[pl.ds(0, n), :].astype(F32) + got_ref[pl.ds(0, n), :].astype(F32)
    unit, rstd = norm_of(x_ref[...])
    scaled = gradient * weight_ref[...]
    inner = jnp.mean(scaled * unit, axis=-1, keepdims=True)
    out_ref[...] = (og_ref[...].astype(F32) + rstd * (scaled - unit * inner)).astype(BF16)
    g = gain_ref[...] + gain_of(got_ref[pl.ds(n, EXTRA), :])
    for j in range(8):
        for i in range(8):
            sum_ref[i, pl.ds(j, 1), :] = g[:, j * 128 : (j + 1) * 128]


def own_rows(where, inputs, og, weight, gain, mine, got, ties):
    n, depth = mine.shape[0] - EXTRA, mine.shape[1]

    def fixed(shape):
        return pl.BlockSpec(shape, lambda i, c: (0, 0))

    row = pl.BlockSpec((n, depth), lambda i, c: (row_code(c), 0))
    return pl.pallas_call(
        rows_kernel,
        grid_spec=pltpu.PrefetchScalarGridSpec(
            num_scalar_prefetch=1,
            grid=(1,),
            in_specs=[row, row, fixed((1, depth)), fixed((1, depth)), fixed(mine.shape), fixed(got.shape), *[ANYWHERE] * len(ties)],
            out_specs=[fixed((n, depth)), pl.BlockSpec((8, 8, 128), lambda i, c: (0, 0, 0))],
        ),
        out_shape=[jax.ShapeDtypeStruct((n, depth), BF16), jax.ShapeDtypeStruct((8, 8, 128), F32)],
        compiler_params=pltpu.CompilerParams(vmem_limit_bytes=4 << 20),
        cost_estimate=pl.CostEstimate(flops=1 << 10, bytes_accessed=1 << 10, transcendentals=0),
        name="own_rows",
    )(where, inputs, og, weight, gain, mine, got, *ties)


ANYWHERE = pl.BlockSpec(memory_space=pl.ANY)


def place_kernel(late, where, *refs):
    halves, sem = refs[:3], refs[-1]
    outs = refs[7:11] if late else refs[3:7]
    if not late:
        refs[7][...] = jnp.zeros(refs[7].shape, F32)
    named = dict(zip(("query", "key", "value", "out"), outs))
    copies = []
    for i, piece in enumerate(PIECES):
        code = piece_code(where, i)
        for p in range(4 * late, 4 * late + 4):
            for at, name, rows in spans(piece, p, p ^ code, piece_rows(piece)):
                if name == "out":
                    pairs = [(at, 64, named[name].at[rows, pl.ds(0, 512)]), (at + 64, 64, named[name].at[rows, pl.ds(512, 512)])]
                else:
                    pairs = [(at, rows.size, named[name].at[rows, :])]
                for first, n, dst in pairs:
                    copy = pltpu.make_async_copy(halves[i].at[pl.ds(first, n), :], dst, sem.at[len(copies)])
                    copy.start()
                    copies.append(copy)
    for copy in copies:
        copy.wait()


def place(late, where, halves, outs, depth, width):
    shapes = [jax.ShapeDtypeStruct((depth, width), BF16)] * 3 + [jax.ShapeDtypeStruct((width, depth), BF16)]
    return pl.pallas_call(
        functools.partial(place_kernel, late),
        in_specs=[SCALARS, *whole(3), *[ANYWHERE] * len(outs)],
        out_specs=[ANYWHERE] * 4 + whole(1 - late),
        out_shape=shapes + [jax.ShapeDtypeStruct((8, 128), F32)] * (1 - late),
        scratch_shapes=[pltpu.SemaphoreType.DMA((28,))],
        input_output_aliases={4 + i: i for i in range(len(outs))},
        compiler_params=pltpu.CompilerParams(vmem_limit_bytes=4 << 20),
        cost_estimate=pl.CostEstimate(flops=(1 << 36) if late else (1 << 10), bytes_accessed=1 << 10, transcendentals=0),
        name="place_late" if late else "place_early",
    )(where, *halves, *outs)


def place_rows_kernel(where, low_ref, high_ref, out_ref, sem):
    code = row_code(where)
    copies = []
    for p in range(8):
        src = high_ref if p >= 4 else low_ref
        rows = pl.ds(pl.multiple_of((p ^ code) * 64, 64), 64)
        copy = pltpu.make_async_copy(src.at[pl.ds((p % 4) * 64, 64), :], out_ref.at[rows, :], sem.at[p])
        copy.start()
        copies.append(copy)
    for copy in copies:
        copy.wait()


def place_rows(where, low, high):
    return pl.pallas_call(
        place_rows_kernel,
        in_specs=[SCALARS, *whole(2)],
        out_specs=ANYWHERE,
        out_shape=jax.ShapeDtypeStruct((2 * low.shape[0], low.shape[1]), BF16),
        scratch_shapes=[pltpu.SemaphoreType.DMA((8,))],
        compiler_params=pltpu.CompilerParams(vmem_limit_bytes=4 << 20),
        cost_estimate=pl.CostEstimate(flops=1 << 10, bytes_accessed=2 << 20, transcendentals=0),
        name="place_rows",
    )(where, low, high)


def plus(*values):
    total = values[0].astype(F32)
    for value in values[1:]:
        total = total + value.astype(F32)
    return total.astype(BF16)


def after(value, first):
    return lax.optimization_barrier((value, *first))[0]


def shards(
    inputs,
    norm_gain_vector,
    query_saved,
    key_saved,
    value_saved,
    w_query,
    w_key,
    w_value,
    w_out,
    output_gradient,
):
    length, depth = inputs.shape
    width = query_saved.shape[1]
    where = position()
    weight = norm_gain_vector.reshape(1, depth)
    *pieces, gq, gk, gv = front(where, weight, output_gradient, w_out, query_saved, key_saved, value_saved, inputs)
    m_send, m_keep, gain = total_share(where, inputs, gq, gk, gv, w_query, w_key, w_value)

    sends, keeps = pieces[0::2], pieces[1::2]
    sizes = [piece_rows(piece) for piece in PIECES]
    first = [swap(s, o[0]) for s, o in zip(sends, ORDERS)]
    r1 = swap(m_send, "core")
    send, gain = mp_step(gain, (m_keep, r1), 128, 128)
    r2 = swap(send, "g0")
    send, gain = mp_step(gain, (m_keep, r1, r2), 64, 64)
    second = [after(plus(k[2 * n :], r[2 * n :]), [send]) for k, r, n in zip(keeps, first, sizes)]
    r3 = swap(send, "g1")
    received = [swap(v, o[1]) for v, o in zip(second, ORDERS)]
    send, gain = mp_step(gain, (m_keep, r1, r2, r3), 64, 0, second)
    r4 = swap(send, "g2")
    mine = [plus(k[: 2 * n], r[: 2 * n], s) for k, r, s, n in zip(keeps, first, received, sizes)]
    third = [swap(v, o[2]) for v, o in zip(mine, ORDERS)]
    send, gain = mp_step(gain, (send, r4), 64, 0, mine)
    r5 = swap(send, "xh")
    quarter = [plus(v, t) for v, t in zip(mine, third)]
    back = [swap(v, o[1]) for v, o in zip(quarter, ORDERS)]
    half = [jnp.concatenate([v, b]) for v, b in zip(quarter, back)]
    last = [swap(v, o[0]) for v, o in zip(half, ORDERS)]
    rows, gains = own_rows(where, inputs, output_gradient, weight, gain, send, r5, quarter)
    *outs, placed = place(0, where, half, (), depth, width)
    got = swap(rows, "g1")
    rows = jnp.concatenate([after(rows, half), got])
    rows = jnp.concatenate([rows, swap(rows, "g0")])
    gains = lax.all_to_all(after(gains, half), "dp", 0, 0)
    rows = after(rows, last)
    grad_inputs = place_rows(where, rows, swap(rows, "core"))
    outs = place(1, where, last, outs, depth, width)
    return (grad_inputs, *outs, jnp.sum(gains, axis=0).reshape(depth))


def solution(mesh):
    return jax.shard_map(
        shards,
        mesh=mesh,
        in_specs=(
            P("dp", None),
            P(),
            P("dp", "mp"),
            P("dp", "mp"),
            P("dp", "mp"),
            P(None, "mp"),
            P(None, "mp"),
            P(None, "mp"),
            P("mp", None),
            P("dp", None),
        ),
        out_specs=(P("dp", None), P(None, "mp"), P(None, "mp"), P(None, "mp"), P("mp", None), P()),
        check_vma=False,
    )
```
